32 devices in a mesh: groups: 2 (over x), branch: 4 (over y, core), head: 4 (over z).
Axes of the slice: x: 2, y: 2, z: 4, core: 2. Of those that a mesh axis runs over, the one named last changes fastest.
Arguments:
- queries: bfloat16 [128, 8192], P(('groups', 'branch'), 'head'), parts along dimension 0, may hold values from -100 to 100, as said below
- root_keys: bfloat16 [32768, 1024], P(('groups', 'branch'), 'head'), parts along dimension 0, may hold values from -6 to 6
- root_values: bfloat16 [32768, 1024], P(('groups', 'branch'), 'head'), parts along dimension 0, may hold values from -6 to 6
- branch_keys: bfloat16 [8, 4096, 1024], P(('groups', 'branch'), None, 'head'), parts along dimension 0, may hold values from -6 to 6
- branch_values: bfloat16 [8, 4096, 1024], P(('groups', 'branch'), None, 'head'), parts along dimension 0, may hold values from -6 to 6
- branch_lengths: int32 [8], P(('groups', 'branch')), parts along dimension 0, may hold values from 512 to 4096, as said below
- row_branch: int32 [128], P('groups'), parts along dimension 0, may hold values from 0 to 3, as said below
Outputs:
- attended: bfloat16 [128, 8192], P(('groups', 'branch'), 'head'), parts along dimension 0
The draws below stay inside these ranges and needn't reach their ends.
There are 2 independent parts, one for each index of `groups`. The reference program is written for one: setup_inputs(seed, part) draws one part's arguments, and reference() takes and returns one part's arrays. A program takes and returns all parts, laid end to end along the dimension named above; each array names one. Nothing has to cross between parts.
Inputs may be any that keep to these rules, and one draw needn't show every extreme that they name: `queries`: query entries; rows may differ in scale. `row_branch`: no branch has more than 32 rows; some branch has exactly 32. `branch_lengths`: some branch has exactly 4096 live tokens.
All inputs are finite; a program needn't handle non-finite values.
Results may differ from the reference program's by a relative error of at most 0.006.
Values may be sent and summed in bfloat16 or wider, within the bound.
A program may use at most 128 MiB of HBM per device.

```python
import jax
import jax.numpy as jnp
from jax import lax

QHEADS = 64
KVHEADS = 8
HD = 128
BMAX = 4096
BRANCHES = 4
ROWS = 64
MOST = 32
ROOT = 16384


def draw_queries(key, part):
    first = jax.random.fold_in(jax.random.fold_in(key, 5), 0)
    base = 3.0 * jax.random.normal(first, (ROWS, QHEADS * HD), jnp.float32)
    return jnp.clip(base, -15.0, 15.0).astype(jnp.bfloat16)


def draw_row_branch(key, part):
    first, second, third = jax.random.split(jax.random.fold_in(key, 11), 3)
    heavy = jax.random.randint(first, (), 0, BRANCHES)
    slots = jnp.arange((BRANCHES - 1) * MOST, dtype=jnp.int32) // MOST
    slots = slots + (slots >= heavy).astype(jnp.int32)
    chosen = jax.random.permutation(second, slots)[:ROWS - MOST]
    assigned = jnp.concatenate([jnp.full((MOST,), heavy, jnp.int32), chosen])
    return jax.random.permutation(third, assigned).astype(jnp.int32)


def draw_branch_lengths(key, part):
    first, second = jax.random.split(jax.random.fold_in(key, 23))
    lengths = jax.random.randint(first, (BRANCHES,), BMAX // 8, BMAX + 1)
    longest = jax.random.randint(second, (), 0, BRANCHES)
    return jnp.where(jnp.arange(BRANCHES) == longest, BMAX, lengths).astype(jnp.int32)


def steps_of(key, dims, cuts, least, top_value):
    gain = 1.0
    for position, shards_of in cuts:
        draws = jax.random.uniform(jax.random.fold_in(jax.random.fold_in(key, 6), position), (shards_of,), jnp.float32, least / len(cuts), top_value / len(cuts))
        gain = gain * jnp.repeat(jnp.exp(draws), dims[position] // shards_of).reshape((-1,) + (1,) * (len(dims) - 1 - position))
    return gain


def noise(stream_key, dims, spread, most, cuts=(), kind=jnp.bfloat16):
    level = steps_of(stream_key, dims, cuts, -0.22, 0.18) if cuts else 1.0
    values = jax.random.normal(stream_key, dims, jnp.float32) * spread * level
    return jnp.minimum(jnp.maximum(values, -most), most).astype(kind)


def setup_inputs(seed: int = 0, part: int = 0) -> dict:
    streams_of = jax.random.split(jax.random.key(seed), 8)
    part_keys = jax.random.split(jax.random.fold_in(streams_of[7], part), 8)
    queries = draw_queries(jax.random.fold_in(jax.random.fold_in(streams_of[7], part), 71), part)
    root_keys = noise(part_keys[1], (ROOT, KVHEADS * HD), 1.0, 6.0, ((0, 4), (1, 4)))
    root_values = noise(part_keys[2], (ROOT, KVHEADS * HD), 1.0, 6.0, ((0, 4), (1, 4)))
    branch_keys = noise(part_keys[3], (BRANCHES, BMAX, KVHEADS * HD), 1.0, 6.0, ((0, 4), (2, 4)))
    branch_values = noise(part_keys[4], (BRANCHES, BMAX, KVHEADS * HD), 1.0, 6.0, ((0, 4), (2, 4)))
    branch_lengths = draw_branch_lengths(jax.random.fold_in(jax.random.fold_in(streams_of[7], part), 71), part)
    row_branch = draw_row_branch(jax.random.fold_in(jax.random.fold_in(streams_of[7], part), 71), part)
    return {"queries": queries, "root_keys": root_keys, "root_values": root_values, "branch_keys": branch_keys, "branch_values": branch_values, "branch_lengths": branch_lengths, "row_branch": row_branch}


NEG = -1.0e30


def empty_part(count):
    return (jnp.full((count, QHEADS), NEG, jnp.float32), jnp.zeros((count, QHEADS), jnp.float32), jnp.zeros((count, QHEADS, HD), jnp.float32))


def combine(first, second):
    peak = jnp.maximum(first[0], second[0])
    scale_a = jnp.exp(first[0] - peak)
    scale_b = jnp.exp(second[0] - peak)
    return (peak, first[1] * scale_a + second[1] * scale_b, first[2] * scale_a[..., None] + second[2] * scale_b[..., None])


def partial_block(query, keys, values, valid):
    count = query.shape[0]
    scores = jnp.einsum("rgph,bgh->rgpb", query.astype(jnp.float32), keys.astype(jnp.float32)) * (HD ** -0.5)
    scores = jnp.where(valid, scores, NEG)
    peak = jnp.max(scores, axis=-1)
    weights = jnp.where(valid, jnp.exp(scores - peak[..., None]), 0.0)
    total = jnp.sum(weights, axis=-1)
    rounded = lax.optimization_barrier(weights.astype(jnp.bfloat16)).astype(jnp.float32)
    mixed = jnp.einsum("rgpb,bgh->rgph", rounded, values.astype(jnp.float32))
    return (peak.reshape(count, QHEADS), total.reshape(count, QHEADS), mixed.reshape(count, QHEADS, HD))


def reference(queries, root_keys, root_values, branch_keys, branch_values, branch_lengths, row_branch):
    per_group = QHEADS // KVHEADS
    query = queries.reshape(ROWS, KVHEADS, per_group, HD)
    block = min(512, ROOT)
    root_k = root_keys.reshape(ROOT // block, block, KVHEADS, HD)
    root_v = root_values.reshape(ROOT // block, block, KVHEADS, HD)

    def root_step(carry, pair):
        return combine(carry, partial_block(query, pair[0], pair[1], jnp.ones((block,), dtype=bool))), None

    root_part, _ = lax.scan(root_step, empty_part(ROWS), (root_k, root_v))
    inner = min(512, BMAX)
    slot_ids = jnp.arange(MOST, dtype=jnp.int32)
    positions = jnp.arange(BMAX, dtype=jnp.int32).reshape(BMAX // inner, inner)

    def branch_step(carry, index):
        member = row_branch == index
        ranking = jnp.cumsum(member.astype(jnp.int32)) - 1
        picker = member[None, :] & (ranking[None, :] == slot_ids[:, None])
        pick = picker.astype(jnp.float32)
        chosen = jnp.dot(pick, queries.astype(jnp.float32), precision=lax.Precision.HIGHEST).reshape(MOST, KVHEADS, per_group, HD)
        keys = lax.dynamic_index_in_dim(branch_keys, index, 0, keepdims=False).reshape(BMAX // inner, inner, KVHEADS, HD)
        values = lax.dynamic_index_in_dim(branch_values, index, 0, keepdims=False).reshape(BMAX // inner, inner, KVHEADS, HD)
        length = lax.dynamic_index_in_dim(branch_lengths, index, 0, keepdims=False)

        def key_step(state, triple):
            return combine(state, partial_block(chosen, triple[0], triple[1], triple[2] < length)), None

        part, _ = lax.scan(key_step, empty_part(MOST), (keys, values, positions))
        spread_peak = jnp.max(jnp.where(picker[:, :, None], part[0][:, None, :], NEG), axis=0)
        spread_total = jnp.einsum("sr,sk->rk", pick, part[1], precision=lax.Precision.HIGHEST)
        spread_mixed = jnp.einsum("sr,sk->rk", pick, part[2].reshape(MOST, QHEADS * HD), precision=lax.Precision.HIGHEST)
        return combine(carry, (spread_peak, spread_total, spread_mixed.reshape(ROWS, QHEADS, HD))), None

    branch_part, _ = lax.scan(branch_step, empty_part(ROWS), jnp.arange(BRANCHES, dtype=jnp.int32))
    peak, total, mixed = combine(root_part, branch_part)
    return (mixed / total[..., None]).reshape(ROWS, QHEADS * HD).astype(jnp.bfloat16)
```

```python
import functools
import math

import jax
import jax.numpy as jnp
from jax import lax
from jax.experimental import pallas as pl
from jax.experimental.pallas import tpu as pltpu
from jax.sharding import PartitionSpec as P

HD = 128
PER = 8
NEG = -1e30
STAT = 16
MESH = pl.DeviceIdType.MESH
BF = jnp.bfloat16
F32 = jnp.float32
SPLIT_DIMS = (((1,), (1,)), ((), ()))


def split(value, parts):
    pieces = []
    for _ in range(parts):
        piece = value.astype(BF)
        pieces.append(piece)
        value = value - piece.astype(F32)
    return pieces


def kernel(
    n, rows, tokens, groups, tb,
    q_ref, rb_ref, len_ref, rk_ref, rv_ref, bk_ref, bv_ref, out_ref,
    qall, kbuf, vbuf, vt, sbuf0, sbuf1, mbuf0, mbuf1, rnum, rm, right, place_e, rbuf, lbuf,
    send, recv,
    kv_sem, small_sem, q_send, q_recv, o_send, o_recv,
):
    me = lax.axis_index("branch")
    slots = 2 * rows
    cols = slots * PER
    part = rows * PER
    chunks = n // 2
    all_rows = n * rows
    sbufs, mbufs = (sbuf0, sbuf1), (mbuf0, mbuf1)
    factor = math.log2(math.e) / math.sqrt(HD)

    copies = [
        pltpu.make_async_copy(src, dst, kv_sem.at[i])
        for i, (src, dst) in enumerate((
            (rk_ref, kbuf.at[0]), (rv_ref, vbuf.at[0]),
            (bk_ref.at[0], kbuf.at[1]), (bv_ref.at[0], vbuf.at[1]),
        ))
    ]
    own = pltpu.make_async_copy(q_ref, qall.at[me], small_sem.at[0])
    rb_copy = pltpu.make_async_copy(rb_ref, rbuf, small_sem.at[1])
    len_copy = pltpu.make_async_copy(len_ref, lbuf, small_sem.at[2])
    own.start()
    rb_copy.start()
    len_copy.start()
    copies[0].start()

    barrier = pltpu.get_barrier_semaphore()
    for off in range(1, n):
        peer = me ^ off
        pl.semaphore_signal(barrier, inc=1, device_id={"branch": peer}, device_id_type=MESH)
    copies[1].start()
    rb_copy.wait()
    len_copy.wait()
    rb = rbuf[...]
    mem_row = jnp.where(rb == me, 1.0, 0.0).astype(F32)
    r_sub = lax.broadcasted_iota(jnp.int32, (all_rows, all_rows), 0)
    r_lane = lax.broadcasted_iota(jnp.int32, (all_rows, all_rows), 1)
    mem_b = jnp.broadcast_to(mem_row, (all_rows, all_rows))
    mem_col = jnp.sum(jnp.where(r_sub == r_lane, mem_b, 0.0), axis=1, keepdims=True)
    mem_cb = jnp.broadcast_to(mem_col, (all_rows, all_rows))
    rank_row = jnp.sum(jnp.where(r_sub < r_lane, mem_cb, 0.0), axis=0, keepdims=True)
    slot_sub = lax.broadcasted_iota(jnp.int32, (slots, all_rows), 0).astype(F32)
    picker = jnp.where(
        (jnp.broadcast_to(rank_row, (slots, all_rows)) == slot_sub)
        & (jnp.broadcast_to(mem_row, (slots, all_rows)) > 0.5), 1.0, 0.0,
    ).astype(BF)
    sub = lax.broadcasted_iota(jnp.int32, (cols, part), 0)
    lane = lax.broadcasted_iota(jnp.int32, (cols, part), 1)
    same = (sub // slots) == (lane // rows)
    t_sub = lax.broadcasted_iota(jnp.int32, (all_rows, part), 0)
    t_lane = lax.broadcasted_iota(jnp.int32, (all_rows, part), 1)
    for d in range(n):
        spread = jnp.where(t_sub == d * rows + lax.rem(t_lane, rows), 1.0, 0.0).astype(BF)
        wide = jnp.dot(picker, spread, preferred_element_type=F32)
        wide = jnp.concatenate([wide] * PER, axis=0)
        place_e[d] = jnp.where(same, wide, 0.0).astype(BF)
    length = jnp.full((8, cols), lbuf[0], jnp.int32)

    own.wait()
    pl.semaphore_wait(barrier, n - 1)

    q_copies = {}
    for g in range(groups):
        for off in range(1, n):
            peer = me ^ off
            lanes = pl.ds(g * PER * HD, PER * HD)
            copy = pltpu.make_async_remote_copy(
                src_ref=qall.at[me, :, lanes], dst_ref=qall.at[me, :, lanes],
                send_sem=q_send.at[g, off], recv_sem=q_recv.at[g, off],
                device_id={"branch": peer}, device_id_type=MESH,
            )
            copy.start()
            q_copies[g, off] = copy
    copies[2].start()
    copies[3].start()

    def stack(q):
        return jnp.concatenate([q[:, p * HD:(p + 1) * HD] for p in range(PER)], axis=0)

    tasks = [(0, g, 0) for g in range(groups)]
    for g in range(groups):
        tasks += [(1, g, 0)] + [(0, g, k) for k in range(1, chunks)]

    waited = set()

    def once(key, fn):
        if key not in waited:
            waited.add(key)
            fn()

    def need_q(g, off):
        if off > 0:
            once(("q", g, off), q_copies[g, off].wait_recv)

    def stage(first, second, slot):
        other = 1 - slot
        if first is not None:
            src, g, k = first
            lanes = slice(g * PER * HD, (g + 1) * PER * HD)
            once(2 * src, copies[2 * src].wait)
            if src == 0:
                need_q(g, 2 * k)
                need_q(g, 2 * k + 1)
                base = (me // 2) ^ k
                query = jnp.concatenate(
                    [stack(qall[base * 2 + i, :, lanes]) for i in range(2)], axis=0
                )
            else:
                for off in range(n):
                    need_q(g, off)
                whole = qall[:, :, lanes].reshape(all_rows, PER * HD)
                query = stack(jnp.dot(picker, whole, preferred_element_type=F32).astype(BF))
        run = jnp.full((8, cols), NEG, F32)
        total = jnp.zeros((HD + STAT, cols), F32)
        if second is not None:
            src2, g2, k2 = second
            once(2 * src2 + 1, copies[2 * src2 + 1].wait)
            peak = jnp.max(mbufs[other][...], axis=0, keepdims=True) * factor
            top = jnp.broadcast_to(peak, (8, cols))
            fresh = ("vt", src2, g2) not in waited

        for start in range(0, tokens, tb):
            tile = slice(start, start + tb)
            if first is not None:
                keys = kbuf[src, tile, g * HD:(g + 1) * HD]
                score = lax.dot_general(keys, query, SPLIT_DIMS, preferred_element_type=F32)
                score = score.reshape(tb // 8, 8, cols)
                if src == 1:
                    place = start + 8 * lax.broadcasted_iota(jnp.int32, (tb // 8, 8, cols), 0)
                    place = place + lax.broadcasted_iota(jnp.int32, (tb // 8, 8, cols), 1)
                    score = jnp.where(place < length[None], score, NEG)
                run = jnp.maximum(run, jnp.max(score, axis=0))
                sbufs[slot][tile] = score.reshape(tb, cols)
            if second is not None:
                s2 = sbufs[other][tile].reshape(tb // 8, 8, cols)
                weights = jnp.exp2(s2 * factor - top[None]).reshape(tb, cols).astype(BF)
                if fresh:
                    v = jnp.transpose(vbuf[src2, tile, g2 * HD:(g2 + 1) * HD])
                    if src2 == 0 and chunks > 1:
                        vt[g2, :, tile] = v
                else:
                    v = vt[g2, :, tile]
                left = jnp.concatenate([v, jnp.ones((STAT, tb), BF)], axis=0)
                total = total + jnp.dot(left, weights, preferred_element_type=F32)

        if first is not None:
            mbufs[slot][...] = run
        if second is not None:
            waited.add(("vt", src2, g2))
            if src2 == 0:
                rnum[g2, k2] = total
                rm[g2, k2] = top
            else:
                hi, lo = split(total[:HD], 2)
                stats = split(total[HD:HD + 1], 2) + split(peak, 3)
                stats += [jnp.zeros((1, cols), BF)] * (STAT - 5)
                right[g2] = jnp.concatenate([hi, lo] + stats, axis=0)

    sent = []

    def finish(g, k):
        base = (me // 2) ^ k
        e = jnp.concatenate([place_e[base * 2], place_e[base * 2 + 1]], axis=1)
        has = jnp.sum(e.astype(F32), axis=0, keepdims=True) > 0.5
        back = jnp.dot(right[g], e, preferred_element_type=F32)
        b_num = back[:HD] + back[HD:2 * HD]
        b_tot = back[2 * HD:2 * HD + 1] + back[2 * HD + 1:2 * HD + 2]
        b_top = back[2 * HD + 2:2 * HD + 3] + back[2 * HD + 3:2 * HD + 4] + back[2 * HD + 4:2 * HD + 5]
        b_top = jnp.where(has, b_top, NEG)
        r_num = rnum[g, k, :HD]
        r_tot = rnum[g, k, HD:HD + 1]
        r_top = rm[g, k, :1]
        peak = jnp.maximum(r_top, b_top)
        x = jnp.exp2(r_top - peak)
        y = jnp.exp2(b_top - peak)
        tot = r_tot * x + b_tot * y
        inverse = 1.0 / tot
        out = (r_num * (x * inverse) + b_num * (y * inverse)).astype(BF)
        lse = split(peak + jnp.log2(tot), 3)
        lse = jnp.concatenate(lse + [jnp.zeros((1, cols), BF)] * (STAT - 3), axis=0)
        for half in range(2):
            lo, hi = half * part, (half + 1) * part
            send[g, 2 * k + half, :HD] = out[:, lo:hi]
            send[g, 2 * k + half, HD:] = lse[:, lo:hi]
        for off in range(max(1, 2 * k), 2 * k + 2):
            peer = me ^ off
            index = 2 * k + lax.rem(peer, 2)
            copy = pltpu.make_async_remote_copy(
                src_ref=send.at[g, index], dst_ref=recv.at[g, off],
                send_sem=o_send.at[g, off], recv_sem=o_recv.at[g, off],
                device_id={"branch": peer}, device_id_type=MESH,
            )
            copy.start()
            sent.append((g, off, copy))

    def collect(g):
        blocks_in = [send[g, lax.rem(me, 2)]]
        for gg, off, copy in sent:
            if gg == g:
                copy.wait_recv()
                blocks_in.append(recv[g, off])
        lses, outs = [], []
        for block in blocks_in:
            stat = block[HD:].astype(F32)
            lses.append(stat[0:1] + stat[1:2] + stat[2:3])
            outs.append(block[:HD].astype(F32))
        peak = functools.reduce(jnp.maximum, lses)
        scales = [jnp.exp2(line - peak) for line in lses]
        inverse = 1.0 / functools.reduce(jnp.add, scales)
        result = functools.reduce(
            jnp.add, [o * (scale * inverse) for o, scale in zip(outs, scales)]
        )
        result = jnp.transpose(result).astype(BF)
        for p in range(PER):
            out_ref[:, (g * PER + p) * HD:(g * PER + p + 1) * HD] = result[p * rows:(p + 1) * rows]

    previous = None
    done, finished = set(), set()
    for t, task in enumerate(tasks + [None]):
        stage(task, previous, t % 2)
        if previous is not None:
            done.add(previous)
            for g in range(groups):
                for k in reversed(range(chunks)):
                    if (1, g, 0) in done and (0, g, k) in done and (g, k) not in finished:
                        finished.add((g, k))
                        finish(g, k)
        previous = task
    for g in range(groups):
        collect(g)
    for copy in q_copies.values():
        copy.wait_send()
    for _, _, copy in sent:
        copy.wait_send()


def on_device(
    queries, root_keys, root_values, branch_keys, branch_values, branch_lengths, row_branch
):
    rows = queries.shape[0]
    all_rows = row_branch.shape[0]
    n = all_rows // rows
    tokens, width = root_keys.shape
    groups = width // HD
    chunks = n // 2
    slots = 2 * rows
    cols = slots * PER
    part = rows * PER
    tb = min(TB, tokens)
    vmem = pl.BlockSpec(memory_space=pltpu.VMEM)
    hbm = pl.BlockSpec(memory_space=pl.ANY)
    dma = pltpu.SemaphoreType.DMA
    return pl.pallas_call(
        functools.partial(kernel, n, rows, tokens, groups, tb),
        out_shape=pltpu.VMEM(queries.shape, BF),
        in_specs=[hbm] * 7,
        out_specs=vmem,
        scratch_shapes=[
            pltpu.VMEM((n, rows, groups * PER * HD), BF),
            pltpu.VMEM((2, tokens, width), BF),
            pltpu.VMEM((2, tokens, width), BF),
            pltpu.VMEM((groups, HD, tokens), BF),
            pltpu.VMEM((tokens, cols), F32),
            pltpu.VMEM((tokens, cols), F32),
            pltpu.VMEM((8, cols), F32),
            pltpu.VMEM((8, cols), F32),
            pltpu.VMEM((groups, chunks, HD + STAT, cols), F32),
            pltpu.VMEM((groups, chunks, 8, cols), F32),
            pltpu.VMEM((groups, 2 * HD + STAT, cols), BF),
            pltpu.VMEM((n, cols, part), BF),
            pltpu.VMEM((1, all_rows), jnp.int32),
            pltpu.SMEM((1,), jnp.int32),
            pltpu.VMEM((groups, n, HD + STAT, part), BF),
            pltpu.VMEM((groups, n, HD + STAT, part), BF),
            dma((4,)), dma((3,)), dma((groups, n)), dma((groups, n)),
            dma((groups, n)), dma((groups, n)),
        ],
        compiler_params=pltpu.CompilerParams(
            collective_id=0, has_side_effects=True, vmem_limit_bytes=60 * 1024 * 1024
        ),
        name="cascade",
    )(
        queries, row_branch.reshape(1, all_rows), branch_lengths,
        root_keys, root_values, branch_keys, branch_values,
    )


TB = 256


def solution(mesh):
    placed = (
        P(("groups", "branch"), "head"),
        P(("groups", "branch"), "head"),
        P(("groups", "branch"), "head"),
        P(("groups", "branch"), None, "head"),
        P(("groups", "branch"), None, "head"),
        P(("groups", "branch")),
        P("groups"),
    )
    return jax.shard_map(
        on_device,
        mesh=mesh,
        in_specs=placed,
        out_specs=P(("groups", "branch"), "head"),
        check_vma=False,
    )
```

```python
import functools
import math

import jax
import jax.numpy as jnp
from jax import lax
from jax.experimental import pallas as pl
from jax.experimental.pallas import tpu as pltpu
from jax.sharding import PartitionSpec as P

HD = 128
PER = 8
NEG = -1e30
STAT = 16
CHAIN = 32
MESH = pl.DeviceIdType.MESH
BF = jnp.bfloat16
F32 = jnp.float32
SPLIT_DIMS = (((1,), (1,)), ((), ()))


def split(value, parts):
    pieces = []
    for _ in range(parts):
        piece = value.astype(BF)
        pieces.append(piece)
        value = value - piece.astype(F32)
    return pieces


def kernel(
    n, rows, tokens, groups, tb,
    q_ref, rb_ref, len_ref, rk_ref, rv_ref, bk_ref, bv_ref, out_ref,
    qall, kbuf, vbuf, vt, sbuf0, sbuf1, mbuf0, mbuf1, rnum, rm, right, place_e, rbuf, lbuf,
    send, recv,
    kv_sem, small_sem, fence, q_send, q_recv, o_send, o_recv,
):
    me = lax.axis_index("branch")
    slots = 2 * rows
    cols = slots * PER
    part = rows * PER
    chunks = n // 2
    all_rows = n * rows
    sbufs, mbufs = (sbuf0, sbuf1), (mbuf0, mbuf1)
    factor = math.log2(math.e) / math.sqrt(HD)

    copies = [
        pltpu.make_async_copy(src, dst, kv_sem.at[i])
        for i, (src, dst) in enumerate((
            (rk_ref, kbuf.at[0]), (rv_ref, vbuf.at[0]),
            (bk_ref.at[0], kbuf.at[1]), (bv_ref.at[0], vbuf.at[1]),
        ))
    ]
    own = pltpu.make_async_copy(q_ref, qall.at[me], small_sem.at[0])
    rb_copy = pltpu.make_async_copy(rb_ref, rbuf, small_sem.at[1])
    len_copy = pltpu.make_async_copy(len_ref, lbuf, small_sem.at[2])
    own.start()
    rb_copy.start()
    len_copy.start()
    copies[0].start()

    barrier = pltpu.get_barrier_semaphore()
    for off in range(1, n):
        peer = me ^ off
        pl.semaphore_signal(barrier, inc=1, device_id={"branch": peer}, device_id_type=MESH)
    copies[1].start()
    rb_copy.wait()
    len_copy.wait()
    rb = rbuf[...]
    mem_row = jnp.where(rb == me, 1.0, 0.0).astype(F32)
    r_sub = lax.broadcasted_iota(jnp.int32, (all_rows, all_rows), 0)
    r_lane = lax.broadcasted_iota(jnp.int32, (all_rows, all_rows), 1)
    mem_b = jnp.broadcast_to(mem_row, (all_rows, all_rows))
    mem_col = jnp.sum(jnp.where(r_sub == r_lane, mem_b, 0.0), axis=1, keepdims=True)
    mem_cb = jnp.broadcast_to(mem_col, (all_rows, all_rows))
    rank_row = jnp.sum(jnp.where(r_sub < r_lane, mem_cb, 0.0), axis=0, keepdims=True)
    slot_sub = lax.broadcasted_iota(jnp.int32, (slots, all_rows), 0).astype(F32)
    picker = jnp.where(
        (jnp.broadcast_to(rank_row, (slots, all_rows)) == slot_sub)
        & (jnp.broadcast_to(mem_row, (slots, all_rows)) > 0.5), 1.0, 0.0,
    ).astype(BF)
    sub = lax.broadcasted_iota(jnp.int32, (cols, part), 0)
    lane = lax.broadcasted_iota(jnp.int32, (cols, part), 1)
    same = (sub // slots) == (lane // rows)
    t_sub = lax.broadcasted_iota(jnp.int32, (all_rows, part), 0)
    t_lane = lax.broadcasted_iota(jnp.int32, (all_rows, part), 1)
    for d in range(n):
        spread = jnp.where(t_sub == d * rows + lax.rem(t_lane, rows), 1.0, 0.0).astype(BF)
        wide = jnp.dot(picker, spread, preferred_element_type=F32)
        wide = jnp.concatenate([wide] * PER, axis=0)
        place_e[d] = jnp.where(same, wide, 0.0).astype(BF)
    length = jnp.full((8, cols), lbuf[0], jnp.int32)

    own.wait()
    pl.semaphore_wait(barrier, n - 1)

    q_copies = {}
    for g in range(groups):
        for off in range(1, n):
            peer = me ^ off
            lanes = pl.ds(g * PER * HD, PER * HD)
            copy = pltpu.make_async_remote_copy(
                src_ref=qall.at[me, :, lanes], dst_ref=qall.at[me, :, lanes],
                send_sem=q_send.at[g, off], recv_sem=q_recv.at[g, off],
                device_id={"branch": peer}, device_id_type=MESH,
            )
            copy.start()
            q_copies[g, off] = copy
    copies[2].start()
    copies[3].start()

    def stack(q):
        return jnp.concatenate([q[:, p * HD:(p + 1) * HD] for p in range(PER)], axis=0)

    tasks = [(0, g, 0) for g in range(groups)]
    for g in range(groups):
        tasks += [(1, g, 0)] + [(0, g, k) for k in range(1, chunks)]

    waited = set()

    def once(key, fn):
        if key not in waited:
            waited.add(key)
            fn()

    def need_q(g, off):
        if off > 0:
            once(("q", g, off), q_copies[g, off].wait_recv)

    def stage(first, second, slot):
        other = 1 - slot
        pl.semaphore_signal(fence, inc=1)
        pl.semaphore_wait(fence, 1)
        if first is not None:
            src, g, k = first
            lanes = slice(g * PER * HD, (g + 1) * PER * HD)
            once(2 * src, copies[2 * src].wait)
            if src == 0:
                need_q(g, 2 * k)
                need_q(g, 2 * k + 1)
                base = (me // 2) ^ k
                query = jnp.concatenate(
                    [stack(qall[base * 2 + i, :, lanes]) for i in range(2)], axis=0
                )
            else:
                for off in range(n):
                    need_q(g, off)
                whole = qall[:, :, lanes].reshape(all_rows, PER * HD)
                query = stack(jnp.dot(picker, whole, preferred_element_type=F32).astype(BF))
        run = jnp.full((CHAIN, cols), NEG, F32)
        total = jnp.zeros((HD + STAT, cols), F32)
        if second is not None:
            src2, g2, k2 = second
            once(2 * src2 + 1, copies[2 * src2 + 1].wait)
            peak = jnp.max(mbufs[other][...], axis=0, keepdims=True) * factor
            top = jnp.broadcast_to(peak, (8, cols))
            fresh = ("vt", src2, g2) not in waited

        for start in range(0, tokens, tb):
            tile = slice(start, start + tb)
            if first is not None:
                keys = kbuf[src, tile, g * HD:(g + 1) * HD]
                score = lax.dot_general(keys, query, SPLIT_DIMS, preferred_element_type=F32)
                score = score.reshape(tb // 8, 8, cols)
                if src == 1:
                    place = start + 8 * lax.broadcasted_iota(jnp.int32, (tb // 8, 8, cols), 0)
                    place = place + lax.broadcasted_iota(jnp.int32, (tb // 8, 8, cols), 1)
                    score = jnp.where(place < length[None], score, NEG)
                run = jnp.maximum(run, jnp.max(score.reshape(tb // CHAIN, CHAIN, cols), axis=0))
                sbufs[slot][tile] = score.reshape(tb, cols)
            if second is not None:
                s2 = sbufs[other][tile].reshape(tb // 8, 8, cols)
                weights = jnp.exp2(s2 * factor - top[None]).reshape(tb, cols).astype(BF)
                if fresh:
                    v = jnp.transpose(vbuf[src2, tile, g2 * HD:(g2 + 1) * HD])
                    if src2 == 0 and chunks > 1:
                        vt[g2, :, tile] = v
                else:
                    v = vt[g2, :, tile]
                left = jnp.concatenate([v, jnp.ones((STAT, tb), BF)], axis=0)
                total = total + jnp.dot(left, weights, preferred_element_type=F32)

        if first is not None:
            mbufs[slot][...] = run
        if second is not None:
            waited.add(("vt", src2, g2))
            if src2 == 0:
                rnum[g2, k2] = total
                rm[g2, k2] = top
            else:
                hi, lo = split(total[:HD], 2)
                stats = split(total[HD:HD + 1], 2) + split(peak, 3)
                stats += [jnp.zeros((1, cols), BF)] * (STAT - 5)
                right[g2] = jnp.concatenate([hi, lo] + stats, axis=0)

    sent = []

    def finish(g, k):
        base = (me // 2) ^ k
        e = jnp.concatenate([place_e[base * 2], place_e[base * 2 + 1]], axis=1)
        has = jnp.sum(e.astype(F32), axis=0, keepdims=True) > 0.5
        back = jnp.dot(right[g], e, preferred_element_type=F32)
        b_num = back[:HD] + back[HD:2 * HD]
        b_tot = back[2 * HD:2 * HD + 1] + back[2 * HD + 1:2 * HD + 2]
        b_top = back[2 * HD + 2:2 * HD + 3] + back[2 * HD + 3:2 * HD + 4] + back[2 * HD + 4:2 * HD + 5]
        b_top = jnp.where(has, b_top, NEG)
        r_num = rnum[g, k, :HD]
        r_tot = rnum[g, k, HD:HD + 1]
        r_top = rm[g, k, :1]
        peak = jnp.maximum(r_top, b_top)
        x = jnp.exp2(r_top - peak)
        y = jnp.exp2(b_top - peak)
        tot = r_tot * x + b_tot * y
        inverse = 1.0 / tot
        out = (r_num * (x * inverse) + b_num * (y * inverse)).astype(BF)
        lse = split(peak + jnp.log2(tot), 3)
        lse = jnp.concatenate(lse + [jnp.zeros((1, cols), BF)] * (STAT - 3), axis=0)
        for half in range(2):
            lo, hi = half * part, (half + 1) * part
            send[g, 2 * k + half, :HD] = out[:, lo:hi]
            send[g, 2 * k + half, HD:] = lse[:, lo:hi]
        for off in range(max(1, 2 * k), 2 * k + 2):
            peer = me ^ off
            index = 2 * k + lax.rem(peer, 2)
            copy = pltpu.make_async_remote_copy(
                src_ref=send.at[g, index], dst_ref=recv.at[g, off],
                send_sem=o_send.at[g, off], recv_sem=o_recv.at[g, off],
                device_id={"branch": peer}, device_id_type=MESH,
            )
            copy.start()
            sent.append((g, off, copy))

    def collect(g):
        blocks_in = [send[g, lax.rem(me, 2)]]
        for gg, off, copy in sent:
            if gg == g:
                copy.wait_recv()
                blocks_in.append(recv[g, off])
        lses, outs = [], []
        for block in blocks_in:
            stat = block[HD:].astype(F32)
            lses.append(stat[0:1] + stat[1:2] + stat[2:3])
            outs.append(block[:HD].astype(F32))
        peak = functools.reduce(jnp.maximum, lses)
        scales = [jnp.exp2(line - peak) for line in lses]
        inverse = 1.0 / functools.reduce(jnp.add, scales)
        result = functools.reduce(
            jnp.add, [o * (scale * inverse) for o, scale in zip(outs, scales)]
        )
        result = jnp.transpose(result).astype(BF)
        for p in range(PER):
            out_ref[:, (g * PER + p) * HD:(g * PER + p + 1) * HD] = result[p * rows:(p + 1) * rows]

    previous = None
    done, finished = set(), set()
    for t, task in enumerate(tasks + [None]):
        stage(task, previous, t % 2)
        if previous is not None:
            done.add(previous)
            for g in range(groups):
                for k in reversed(range(chunks)):
                    if (1, g, 0) in done and (0, g, k) in done and (g, k) not in finished:
                        finished.add((g, k))
                        finish(g, k)
        previous = task
    for g in range(groups):
        collect(g)
    for copy in q_copies.values():
        copy.wait_send()
    for _, _, copy in sent:
        copy.wait_send()


def on_device(
    queries, root_keys, root_values, branch_keys, branch_values, branch_lengths, row_branch
):
    rows = queries.shape[0]
    all_rows = row_branch.shape[0]
    n = all_rows // rows
    tokens, width = root_keys.shape
    groups = width // HD
    chunks = n // 2
    slots = 2 * rows
    cols = slots * PER
    part = rows * PER
    tb = min(TB, tokens)
    vmem = pl.BlockSpec(memory_space=pltpu.VMEM)
    hbm = pl.BlockSpec(memory_space=pl.ANY)
    dma = pltpu.SemaphoreType.DMA
    return pl.pallas_call(
        functools.partial(kernel, n, rows, tokens, groups, tb),
        out_shape=pltpu.VMEM(queries.shape, BF),
        in_specs=[hbm] * 7,
        out_specs=vmem,
        scratch_shapes=[
            pltpu.VMEM((n, rows, groups * PER * HD), BF),
            pltpu.VMEM((2, tokens, width), BF),
            pltpu.VMEM((2, tokens, width), BF),
            pltpu.VMEM((groups, HD, tokens), BF),
            pltpu.VMEM((tokens, cols), F32),
            pltpu.VMEM((tokens, cols), F32),
            pltpu.VMEM((CHAIN, cols), F32),
            pltpu.VMEM((CHAIN, cols), F32),
            pltpu.VMEM((groups, chunks, HD + STAT, cols), F32),
            pltpu.VMEM((groups, chunks, 8, cols), F32),
            pltpu.VMEM((groups, 2 * HD + STAT, cols), BF),
            pltpu.VMEM((n, cols, part), BF),
            pltpu.VMEM((1, all_rows), jnp.int32),
            pltpu.SMEM((1,), jnp.int32),
            pltpu.VMEM((groups, n, HD + STAT, part), BF),
            pltpu.VMEM((groups, n, HD + STAT, part), BF),
            dma((4,)), dma((3,)), pltpu.SemaphoreType.REGULAR, dma((groups, n)), dma((groups, n)),
            dma((groups, n)), dma((groups, n)),
        ],
        compiler_params=pltpu.CompilerParams(
            collective_id=0, has_side_effects=True, vmem_limit_bytes=60 * 1024 * 1024
        ),
        name="cascade",
    )(
        queries, row_branch.reshape(1, all_rows), branch_lengths,
        root_keys, root_values, branch_keys, branch_values,
    )


TB = 256


def solution(mesh):
    placed = (
        P(("groups", "branch"), "head"),
        P(("groups", "branch"), "head"),
        P(("groups", "branch"), "head"),
        P(("groups", "branch"), None, "head"),
        P(("groups", "branch"), None, "head"),
        P(("groups", "branch")),
        P("groups"),
    )
    return jax.shard_map(
        on_device,
        mesh=mesh,
        in_specs=placed,
        out_specs=P(("groups", "branch"), "head"),
        check_vma=False,
    )
```

```python
import functools
import math

import jax
import jax.numpy as jnp
from jax import lax
from jax.experimental import pallas as pl
from jax.experimental.pallas import tpu as pltpu
from jax.sharding import PartitionSpec as P

HD = 128
PER = 8
NEG = -1e30
STAT = 16
CHAIN = 32
MESH = pl.DeviceIdType.MESH
BF = jnp.bfloat16
F32 = jnp.float32
SPLIT_DIMS = (((1,), (1,)), ((), ()))


def split(value, parts):
    pieces = []
    for _ in range(parts):
        piece = value.astype(BF)
        pieces.append(piece)
        value = value - piece.astype(F32)
    return pieces


def kernel(
    n, rows, tokens, groups, tb,
    q_ref, rb_ref, len_ref, rk_ref, rv_ref, bk_ref, bv_ref, out_ref,
    qall, qcur, kbuf, vbuf, sbuf, mbuf, pnum, ptop, right, place_e, rbuf, lbuf,
    send, recv,
    kv_sem, small_sem, fence, q_send, q_recv, o_send, o_recv,
):
    me = lax.axis_index("branch")
    slots = 2 * rows
    cols = slots * PER
    part = rows * PER
    chunks = n // 2
    all_rows = n * rows
    factor = math.log2(math.e) / math.sqrt(HD)

    copies = [
        pltpu.make_async_copy(src, dst, kv_sem.at[i])
        for i, (src, dst) in enumerate((
            (rk_ref, kbuf.at[0]), (rv_ref, vbuf.at[0]),
            (bk_ref.at[0], kbuf.at[1]), (bv_ref.at[0], vbuf.at[1]),
        ))
    ]
    own = pltpu.make_async_copy(q_ref, qall.at[me], small_sem.at[0])
    rb_copy = pltpu.make_async_copy(rb_ref, rbuf, small_sem.at[1])
    len_copy = pltpu.make_async_copy(len_ref, lbuf, small_sem.at[2])
    own.start()
    rb_copy.start()
    len_copy.start()
    copies[0].start()

    barrier = pltpu.get_barrier_semaphore()
    for off in range(1, n):
        peer = me ^ off
        pl.semaphore_signal(barrier, inc=1, device_id={"branch": peer}, device_id_type=MESH)
    for copy in copies[1:]:
        copy.start()
    rb_copy.wait()
    len_copy.wait()
    rb = rbuf[...]
    mem_row = jnp.where(rb == me, 1.0, 0.0).astype(F32)
    r_sub = lax.broadcasted_iota(jnp.int32, (all_rows, all_rows), 0)
    r_lane = lax.broadcasted_iota(jnp.int32, (all_rows, all_rows), 1)
    mem_b = jnp.broadcast_to(mem_row, (all_rows, all_rows))
    mem_col = jnp.sum(jnp.where(r_sub == r_lane, mem_b, 0.0), axis=1, keepdims=True)
    mem_cb = jnp.broadcast_to(mem_col, (all_rows, all_rows))
    rank_row = jnp.sum(jnp.where(r_sub < r_lane, mem_cb, 0.0), axis=0, keepdims=True)
    slot_sub = lax.broadcasted_iota(jnp.int32, (slots, all_rows), 0).astype(F32)
    picker = jnp.where(
        (jnp.broadcast_to(rank_row, (slots, all_rows)) == slot_sub)
        & (jnp.broadcast_to(mem_row, (slots, all_rows)) > 0.5), 1.0, 0.0,
    ).astype(BF)
    sub = lax.broadcasted_iota(jnp.int32, (cols, part), 0)
    lane = lax.broadcasted_iota(jnp.int32, (cols, part), 1)
    same = (sub // slots) == (lane // rows)
    t_sub = lax.broadcasted_iota(jnp.int32, (all_rows, part), 0)
    t_lane = lax.broadcasted_iota(jnp.int32, (all_rows, part), 1)
    for d in range(n):
        spread = jnp.where(t_sub == d * rows + lax.rem(t_lane, rows), 1.0, 0.0).astype(BF)
        wide = jnp.dot(picker, spread, preferred_element_type=F32)
        wide = jnp.concatenate([wide] * PER, axis=0)
        place_e[d] = jnp.where(same, wide, 0.0).astype(BF)
    length = jnp.full((8, cols), lbuf[0], jnp.int32)

    own.wait()
    pl.semaphore_wait(barrier, n - 1)

    q_copies = {}
    for g in range(groups):
        for off in range(1, n):
            peer = me ^ off
            lanes = pl.ds(g * PER * HD, PER * HD)
            copy = pltpu.make_async_remote_copy(
                src_ref=qall.at[me, :, lanes], dst_ref=qall.at[me, :, lanes],
                send_sem=q_send.at[g, off], recv_sem=q_recv.at[g, off],
                device_id={"branch": peer}, device_id_type=MESH,
            )
            copy.start()
            q_copies[g, off] = copy

    def stack(q):
        return jnp.concatenate([q[:, p * HD:(p + 1) * HD] for p in range(PER)], axis=0)

    tasks = [(0, g, 0) for g in range(groups)]
    for g in range(groups):
        tasks += [(1, g, 0)] + [(0, g, k) for k in range(1, chunks)]
    place_of = {task: t for t, task in enumerate(tasks)}
    last = len(tasks)

    waited = set()

    def need_q(g, off):
        if off > 0 and (g, off) not in waited:
            waited.add((g, off))
            q_copies[g, off].wait_recv()

    def load_query(t):
        src, g, k = tasks[t]
        lanes = slice(g * PER * HD, (g + 1) * PER * HD)
        if src == 0:
            need_q(g, 2 * k)
            need_q(g, 2 * k + 1)
            base = (me // 2) ^ k
            for i in range(2):
                qcur[i * part:(i + 1) * part] = stack(qall[base * 2 + i, :, lanes])
        else:
            if t == groups:
                copies[2].wait()
                copies[3].wait()
            for off in range(n):
                need_q(g, off)
            whole = qall[:, :, lanes].reshape(all_rows, PER * HD)
            qcur[...] = stack(jnp.dot(picker, whole, preferred_element_type=F32).astype(BF))

    def fence_here():
        pl.semaphore_signal(fence, inc=1)
        pl.semaphore_wait(fence, 1)

    def buffer_of(t):
        late = t - groups
        step = lax.rem(late, chunks)
        first = jnp.where(step == 0, groups + late // chunks, late // chunks)
        return jnp.where(t < groups, t, first)

    def lanes_of(at):
        return pl.ds(pl.multiple_of(lax.rem(at, groups) * HD, HD), HD)

    def stage(t, first, second, masked):
        if first:
            at = buffer_of(t) if masked else jnp.int32(t)
            query = qcur[...]
            limit = jnp.where(at >= groups, length, tokens) if masked else None
        if second:
            at2 = buffer_of(t - 1) if masked else buffer_of(jnp.int32(t - 1))
            peak = jnp.max(mbuf[...], axis=0, keepdims=True) * factor
            top = jnp.broadcast_to(peak, (8, cols))
        run = jnp.full((CHAIN, cols), NEG, F32)
        total = jnp.zeros((HD + STAT, cols), F32)
        for start in range(0, tokens, tb):
            tile = slice(start, start + tb)
            if second:
                s2 = sbuf[tile].reshape(tb // 8, 8, cols)
                weights = jnp.exp2(s2 * factor - top[None]).reshape(tb, cols).astype(BF)
            if first:
                score = lax.dot_general(kbuf[at // groups, tile, lanes_of(at)], query, SPLIT_DIMS, preferred_element_type=F32)
                if masked:
                    score = score.reshape(tb // 8, 8, cols)
                    place = start + 8 * lax.broadcasted_iota(jnp.int32, (tb // 8, 8, cols), 0)
                    place = place + lax.broadcasted_iota(jnp.int32, (tb // 8, 8, cols), 1)
                    score = jnp.where(place < limit[None], score, NEG)
                chains = score.reshape(tb // CHAIN, CHAIN, cols)
                run = jnp.maximum(run, jnp.max(chains, axis=0))
                sbuf[tile] = score.reshape(tb, cols)
            if second:
                v = jnp.transpose(vbuf[at2 // groups, tile, lanes_of(at2)])
                left = jnp.concatenate([v, jnp.ones((STAT, tb), BF)], axis=0)
                total = total + jnp.dot(left, weights, preferred_element_type=F32)
        if first:
            mbuf[...] = run
        if second:
            pnum[t - 1] = total
            ptop[t - 1] = top

    sent = []
    outgoing = {}
    for g in range(groups):
        for off in range(1, n):
            peer = me ^ off
            index = 2 * (off // 2) + lax.rem(peer, 2)
            outgoing[g, off] = pltpu.make_async_remote_copy(
                src_ref=send.at[g, index], dst_ref=recv.at[g, off],
                send_sem=o_send.at[g, off], recv_sem=o_recv.at[g, off],
                device_id={"branch": peer}, device_id_type=MESH,
            )
            sent.append((g, off, outgoing[g, off]))

    def pack_branch(g):
        t = place_of[1, g, 0]
        hi, lo = split(pnum[t, :HD], 2)
        stats = split(pnum[t, HD:HD + 1], 2) + split(ptop[t, :1], 3)
        stats += [jnp.zeros((1, cols), BF)] * (STAT - 5)
        right[g] = jnp.concatenate([hi, lo] + stats, axis=0)

    def finish(g, k):
        base = (me // 2) ^ k
        e = jnp.concatenate([place_e[base * 2], place_e[base * 2 + 1]], axis=1)
        has = jnp.sum(e.astype(F32), axis=0, keepdims=True) > 0.5
        back = jnp.dot(right[g], e, preferred_element_type=F32)
        b_num = back[:HD] + back[HD:2 * HD]
        b_tot = back[2 * HD:2 * HD + 1] + back[2 * HD + 1:2 * HD + 2]
        b_top = back[2 * HD + 2:2 * HD + 3] + back[2 * HD + 3:2 * HD + 4] + back[2 * HD + 4:2 * HD + 5]
        b_top = jnp.where(has, b_top, NEG)
        t = place_of[0, g, k]
        r_num = pnum[t, :HD]
        r_tot = pnum[t, HD:HD + 1]
        r_top = ptop[t, :1]
        peak = jnp.maximum(r_top, b_top)
        x = jnp.exp2(r_top - peak)
        y = jnp.exp2(b_top - peak)
        tot = r_tot * x + b_tot * y
        inverse = 1.0 / tot
        out = (r_num * (x * inverse) + b_num * (y * inverse)).astype(BF)
        lse = split(peak + jnp.log2(tot), 3)
        lse = jnp.concatenate(lse + [jnp.zeros((1, cols), BF)] * (STAT - 3), axis=0)
        for half in range(2):
            lo, hi = half * part, (half + 1) * part
            send[g, 2 * k + half, :HD] = out[:, lo:hi]
            send[g, 2 * k + half, HD:] = lse[:, lo:hi]
        for off in range(max(1, 2 * k), 2 * k + 2):
            outgoing[g, off].start()

    def collect(g):
        blocks_in = [send[g, lax.rem(me, 2)]]
        for gg, off, copy in sent:
            if gg == g:
                copy.wait_recv()
                blocks_in.append(recv[g, off])
        lses, outs = [], []
        for block in blocks_in:
            stat = block[HD:].astype(F32)
            lses.append(stat[0:1] + stat[1:2] + stat[2:3])
            outs.append(block[:HD].astype(F32))
        peak = functools.reduce(jnp.maximum, lses)
        scales = [jnp.exp2(line - peak) for line in lses]
        inverse = 1.0 / functools.reduce(jnp.add, scales)
        result = functools.reduce(
            jnp.add, [o * (scale * inverse) for o, scale in zip(outs, scales)]
        )
        result = jnp.transpose(result).astype(BF)
        for p in range(PER):
            out_ref[:, (g * PER + p) * HD:(g * PER + p + 1) * HD] = result[p * rows:(p + 1) * rows]

    ready = {}
    done, finished = set(), set()
    for t, task in enumerate(tasks):
        done.add(task)
        for g in range(groups):
            for k in reversed(range(chunks)):
                if k > 0 and (1, g, 0) in done and (0, g, k) in done and (g, k) not in finished:
                    finished.add((g, k))
                    ready.setdefault(t, []).append((g, k))

    def settle(t):
        if tasks[t][0] == 1:
            pack_branch(tasks[t][1])
        for g, k in ready.get(t, ()):
            finish(g, k)

    copies[0].wait()
    load_query(0)
    stage(0, True, False, False)
    copies[1].wait()

    def step(t, carry):
        for i in range(1, last):
            pl.when(t == i)(functools.partial(load_query, i))
        fence_here()
        stage(t, True, True, True)
        for i in range(1, last):
            if tasks[i - 1][0] == 1 or ready.get(i - 1):
                pl.when(t == i)(functools.partial(settle, i - 1))
        return carry

    lax.fori_loop(1, last, step, 0)
    stage(last, False, True, False)
    settle(last - 1)
    for g in range(groups):
        finish(g, 0)
    for g in range(groups):
        collect(g)
    for copy in q_copies.values():
        copy.wait_send()
    for _, _, copy in sent:
        copy.wait_send()


def on_device(
    queries, root_keys, root_values, branch_keys, branch_values, branch_lengths, row_branch
):
    rows = queries.shape[0]
    all_rows = row_branch.shape[0]
    n = all_rows // rows
    tokens, width = root_keys.shape
    groups = width // HD
    chunks = n // 2
    slots = 2 * rows
    cols = slots * PER
    part = rows * PER
    tb = min(TB, tokens)
    vmem = pl.BlockSpec(memory_space=pltpu.VMEM)
    hbm = pl.BlockSpec(memory_space=pl.ANY)
    dma = pltpu.SemaphoreType.DMA
    return pl.pallas_call(
        functools.partial(kernel, n, rows, tokens, groups, tb),
        out_shape=pltpu.VMEM(queries.shape, BF),
        in_specs=[hbm] * 7,
        out_specs=vmem,
        scratch_shapes=[
            pltpu.VMEM((n, rows, groups * PER * HD), BF),
            pltpu.VMEM((cols, HD), BF),
            pltpu.VMEM((2, tokens, groups * HD), BF),
            pltpu.VMEM((2, tokens, groups * HD), BF),
            pltpu.VMEM((tokens, cols), F32),
            pltpu.VMEM((CHAIN, cols), F32),
            pltpu.VMEM((groups * (chunks + 1), HD + STAT, cols), F32),
            pltpu.VMEM((groups * (chunks + 1), 8, cols), F32),
            pltpu.VMEM((groups, 2 * HD + STAT, cols), BF),
            pltpu.VMEM((n, cols, part), BF),
            pltpu.VMEM((1, all_rows), jnp.int32),
            pltpu.SMEM((1,), jnp.int32),
            pltpu.VMEM((groups, n, HD + STAT, part), BF),
            pltpu.VMEM((groups, n, HD + STAT, part), BF),
            dma((4,)), dma((3,)), pltpu.SemaphoreType.REGULAR, dma((groups, n)), dma((groups, n)),
            dma((groups, n)), dma((groups, n)),
        ],
        compiler_params=pltpu.CompilerParams(
            collective_id=0, has_side_effects=True, vmem_limit_bytes=60 * 1024 * 1024
        ),
        name="cascade",
    )(
        queries, row_branch.reshape(1, all_rows), branch_lengths,
        root_keys, root_values, branch_keys, branch_values,
    )


TB = 256


def solution(mesh):
    placed = (
        P(("groups", "branch"), "head"),
        P(("groups", "branch"), "head"),
        P(("groups", "branch"), "head"),
        P(("groups", "branch"), None, "head"),
        P(("groups", "branch"), None, "head"),
        P(("groups", "branch")),
        P("groups"),
    )
    return jax.shard_map(
        on_device,
        mesh=mesh,
        in_specs=placed,
        out_specs=P(("groups", "branch"), "head"),
        check_vma=False,
    )
```

```python
import functools
import math

import jax
import jax.numpy as jnp
from jax import lax
from jax.experimental import pallas as pl
from jax.experimental.pallas import tpu as pltpu
from jax.sharding import PartitionSpec as P

HD = 128
PER = 8
NEG = -1e30
STAT = 16
CHAIN = 32
MESH = pl.DeviceIdType.MESH
BF = jnp.bfloat16
F32 = jnp.float32
SPLIT_DIMS = (((1,), (1,)), ((), ()))


def split(value, parts):
    pieces = []
    for _ in range(parts):
        piece = value.astype(BF)
        pieces.append(piece)
        value = value - piece.astype(F32)
    return pieces


def kernel(
    n, rows, tokens, groups, tb,
    q_ref, rb_ref, len_ref, rk_ref, rv_ref, bk_ref, bv_ref, out_ref,
    qall, kbuf, vbuf, vt, sbuf0, sbuf1, mbuf0, mbuf1, rnum, rm, right, place_e, rbuf, lbuf,
    send, recv,
    kv_sem, small_sem, fence, q_send, q_recv, o_send, o_recv,
):
    me = lax.axis_index("branch")
    slots = 2 * rows
    cols = slots * PER
    part = rows * PER
    chunks = n // 2
    span = min(512, tokens)
    all_rows = n * rows
    sbufs, mbufs = (sbuf0, sbuf1), (mbuf0, mbuf1)
    factor = math.log2(math.e) / math.sqrt(HD)

    copies = [
        pltpu.make_async_copy(src, dst, kv_sem.at[i])
        for i, (src, dst) in enumerate((
            (rk_ref, kbuf.at[0]), (rv_ref, vbuf.at[0]),
            (bk_ref.at[0], kbuf.at[1]), (bv_ref.at[0], vbuf.at[1]),
        ))
    ]
    own = pltpu.make_async_copy(q_ref, qall.at[me], small_sem.at[0])
    rb_copy = pltpu.make_async_copy(rb_ref, rbuf, small_sem.at[1])
    len_copy = pltpu.make_async_copy(len_ref, lbuf, small_sem.at[2])
    own.start()
    rb_copy.start()
    len_copy.start()
    copies[0].start()

    barrier = pltpu.get_barrier_semaphore()
    for off in range(1, n):
        peer = me ^ off
        pl.semaphore_signal(barrier, inc=1, device_id={"branch": peer}, device_id_type=MESH)
    copies[1].start()
    rb_copy.wait()
    len_copy.wait()
    rb = rbuf[...]
    mem_row = jnp.where(rb == me, 1.0, 0.0).astype(F32)
    r_sub = lax.broadcasted_iota(jnp.int32, (all_rows, all_rows), 0)
    r_lane = lax.broadcasted_iota(jnp.int32, (all_rows, all_rows), 1)
    mem_b = jnp.broadcast_to(mem_row, (all_rows, all_rows))
    mem_col = jnp.sum(jnp.where(r_sub == r_lane, mem_b, 0.0), axis=1, keepdims=True)
    mem_cb = jnp.broadcast_to(mem_col, (all_rows, all_rows))
    rank_row = jnp.sum(jnp.where(r_sub < r_lane, mem_cb, 0.0), axis=0, keepdims=True)
    slot_sub = lax.broadcasted_iota(jnp.int32, (slots, all_rows), 0).astype(F32)
    picker = jnp.where(
        (jnp.broadcast_to(rank_row, (slots, all_rows)) == slot_sub)
        & (jnp.broadcast_to(mem_row, (slots, all_rows)) > 0.5), 1.0, 0.0,
    ).astype(BF)
    sub = lax.broadcasted_iota(jnp.int32, (cols, part), 0)
    lane = lax.broadcasted_iota(jnp.int32, (cols, part), 1)
    same = (sub // slots) == (lane // rows)
    t_sub = lax.broadcasted_iota(jnp.int32, (all_rows, part), 0)
    t_lane = lax.broadcasted_iota(jnp.int32, (all_rows, part), 1)
    for d in range(n):
        spread = jnp.where(t_sub == d * rows + lax.rem(t_lane, rows), 1.0, 0.0).astype(BF)
        wide = jnp.dot(picker, spread, preferred_element_type=F32)
        wide = jnp.concatenate([wide] * PER, axis=0)
        place_e[d] = jnp.where(same, wide, 0.0).astype(BF)
    length = jnp.full((8, cols), lbuf[0], jnp.int32)

    own.wait()
    pl.semaphore_wait(barrier, n - 1)

    q_copies = {}
    for g in range(groups):
        for off in range(1, n):
            peer = me ^ off
            lanes = pl.ds(g * PER * HD, PER * HD)
            copy = pltpu.make_async_remote_copy(
                src_ref=qall.at[me, :, lanes], dst_ref=qall.at[me, :, lanes],
                send_sem=q_send.at[g, off], recv_sem=q_recv.at[g, off],
                device_id={"branch": peer}, device_id_type=MESH,
            )
            copy.start()
            q_copies[g, off] = copy
    copies[2].start()
    copies[3].start()

    def stack(q):
        return jnp.concatenate([q[:, p * HD:(p + 1) * HD] for p in range(PER)], axis=0)

    tasks = [(0, g, 0) for g in range(groups)]
    for g in range(groups):
        tasks += [(1, g, 0)] + [(0, g, k) for k in range(1, chunks)]

    waited = set()

    def once(key, fn):
        if key not in waited:
            waited.add(key)
            fn()

    def need_q(g, off):
        if off > 0:
            once(("q", g, off), q_copies[g, off].wait_recv)

    def stage(first, second, slot):
        other = 1 - slot
        pl.semaphore_signal(fence, inc=1)
        pl.semaphore_wait(fence, 1)
        if first is not None:
            src, g, k = first
            lanes = slice(g * PER * HD, (g + 1) * PER * HD)
            once(2 * src, copies[2 * src].wait)
            if src == 0:
                need_q(g, 2 * k)
                need_q(g, 2 * k + 1)
                base = (me // 2) ^ k
                query = jnp.concatenate(
                    [stack(qall[base * 2 + i, :, lanes]) for i in range(2)], axis=0
                )
            else:
                for off in range(n):
                    need_q(g, off)
                whole = qall[:, :, lanes].reshape(all_rows, PER * HD)
                query = stack(jnp.dot(picker, whole, preferred_element_type=F32).astype(BF))
        run = jnp.full((CHAIN, cols), NEG, F32)
        total = jnp.zeros((HD + STAT, cols), F32)
        if second is not None:
            src2, g2, k2 = second
            once(2 * src2 + 1, copies[2 * src2 + 1].wait)
            peak = jnp.max(mbufs[other][...], axis=0, keepdims=True) * factor
            top = jnp.broadcast_to(peak, (8, cols))
            fresh = ("vt", src2, g2) not in waited

        for start in range(0, tokens, tb):
            tile = slice(start, start + tb)
            if first is not None:
                keys = kbuf[src, tile, g * HD:(g + 1) * HD]
                score = lax.dot_general(keys, query, SPLIT_DIMS, preferred_element_type=F32)
                score = score.reshape(tb // 8, 8, cols)
                if src == 1:
                    place = start + 8 * lax.broadcasted_iota(jnp.int32, (tb // 8, 8, cols), 0)
                    place = place + lax.broadcasted_iota(jnp.int32, (tb // 8, 8, cols), 1)
                    score = jnp.where(place < length[None], score, NEG)
                run = jnp.maximum(run, jnp.max(score.reshape(tb // CHAIN, CHAIN, cols), axis=0))
                sbufs[slot][tile] = score.reshape(tb, cols)
            if second is not None:
                s2 = sbufs[other][tile].reshape(tb // 8, 8, cols)
                weights = jnp.exp2(s2 * factor - top[None]).reshape(tb, cols).astype(BF)
                if fresh:
                    v = jnp.transpose(vbuf[src2, tile, g2 * HD:(g2 + 1) * HD])
                    if src2 == 0 and chunks > 1:
                        vt[g2, :, tile] = v
                else:
                    v = vt[g2, :, tile]
                left = jnp.concatenate([v, jnp.ones((STAT, tb), BF)], axis=0)
                total = total + jnp.dot(left, weights, preferred_element_type=F32)

        if first is not None:
            mbufs[slot][...] = run
        if second is not None:
            waited.add(("vt", src2, g2))
            if src2 == 0:
                rnum[g2, k2] = total
                rm[g2, k2] = top
            else:
                hi, lo = split(total[:HD], 2)
                stats = split(total[HD:HD + 1], 2) + split(peak, 3)
                stats += [jnp.zeros((1, cols), BF)] * (STAT - 5)
                right[g2] = jnp.concatenate([hi, lo] + stats, axis=0)

    sent = []

    def finish(g, k):
        base = (me // 2) ^ k
        e = jnp.concatenate([place_e[base * 2], place_e[base * 2 + 1]], axis=1)
        has = jnp.sum(e.astype(F32), axis=0, keepdims=True) > 0.5
        back = jnp.dot(right[g], e, preferred_element_type=F32)
        b_num = back[:HD] + back[HD:2 * HD]
        b_tot = back[2 * HD:2 * HD + 1] + back[2 * HD + 1:2 * HD + 2]
        b_top = back[2 * HD + 2:2 * HD + 3] + back[2 * HD + 3:2 * HD + 4] + back[2 * HD + 4:2 * HD + 5]
        b_top = jnp.where(has, b_top, NEG)
        r_num = rnum[g, k, :HD]
        r_tot = rnum[g, k, HD:HD + 1]
        r_top = rm[g, k, :1]
        peak = jnp.maximum(r_top, b_top)
        x = jnp.exp2(r_top - peak)
        y = jnp.exp2(b_top - peak)
        tot = r_tot * x + b_tot * y
        inverse = 1.0 / tot
        out = (r_num * (x * inverse) + b_num * (y * inverse)).astype(BF)
        lse = split(peak + jnp.log2(tot), 3)
        lse = jnp.concatenate(lse + [jnp.zeros((1, cols), BF)] * (STAT - 3), axis=0)
        for half in range(2):
            lo, hi = half * part, (half + 1) * part
            send[g, 2 * k + half, :HD] = out[:, lo:hi]
            send[g, 2 * k + half, HD:] = lse[:, lo:hi]
        for off in range(max(1, 2 * k), 2 * k + 2):
            peer = me ^ off
            index = 2 * k + lax.rem(peer, 2)
            copy = pltpu.make_async_remote_copy(
                src_ref=send.at[g, index], dst_ref=recv.at[g, off],
                send_sem=o_send.at[g, off], recv_sem=o_recv.at[g, off],
                device_id={"branch": peer}, device_id_type=MESH,
            )
            copy.start()
            sent.append((g, off, copy))

    def last_stage(g, k, other):
        for off in (2 * k, 2 * k + 1):
            peer = me ^ off
            lanes = pl.ds(pl.multiple_of(lax.rem(peer, 2) * part, part), part)
            r_top = jnp.max(mbufs[other][:, lanes], axis=0, keepdims=True) * factor
            top = jnp.broadcast_to(r_top, (8, part))
            total = jnp.zeros((HD + STAT, part), F32)
            for start in range(0, tokens, span):
                tile = slice(start, start + span)
                s2 = sbufs[other][tile, lanes].reshape(span // 8, 8, part)
                weights = jnp.exp2(s2 * factor - top[None]).reshape(span, part).astype(BF)
                left = jnp.concatenate([vt[g, :, tile], jnp.ones((STAT, span), BF)], axis=0)
                total = total + jnp.dot(left, weights, preferred_element_type=F32)
            e = place_e[peer]
            has = jnp.sum(e.astype(F32), axis=0, keepdims=True) > 0.5
            back = jnp.dot(right[g], e, preferred_element_type=F32)
            b_num = back[:HD] + back[HD:2 * HD]
            b_tot = back[2 * HD:2 * HD + 1] + back[2 * HD + 1:2 * HD + 2]
            b_top = back[2 * HD + 2:2 * HD + 3] + back[2 * HD + 3:2 * HD + 4] + back[2 * HD + 4:2 * HD + 5]
            b_top = jnp.where(has, b_top, NEG)
            peak = jnp.maximum(r_top, b_top)
            x = jnp.exp2(r_top - peak)
            y = jnp.exp2(b_top - peak)
            tot = total[HD:HD + 1] * x + b_tot * y
            inverse = 1.0 / tot
            out = (total[:HD] * (x * inverse) + b_num * (y * inverse)).astype(BF)
            lse = split(peak + jnp.log2(tot), 3)
            lse = jnp.concatenate(lse + [jnp.zeros((1, part), BF)] * (STAT - 3), axis=0)
            send[g, off, :HD] = out
            send[g, off, HD:] = lse
            copy = pltpu.make_async_remote_copy(
                src_ref=send.at[g, off], dst_ref=recv.at[g, off],
                send_sem=o_send.at[g, off], recv_sem=o_recv.at[g, off],
                device_id={"branch": peer}, device_id_type=MESH,
            )
            copy.start()
            sent.append((g, off, copy))
            pl.semaphore_signal(fence, inc=1)
            pl.semaphore_wait(fence, 1)

    def collect(g):
        blocks_in = [send[g, lax.rem(me, 2)]]
        for gg, off, copy in sent:
            if gg == g:
                copy.wait_recv()
                blocks_in.append(recv[g, off])
        lses, outs = [], []
        for block in blocks_in:
            stat = block[HD:].astype(F32)
            lses.append(stat[0:1] + stat[1:2] + stat[2:3])
            outs.append(block[:HD].astype(F32))
        peak = functools.reduce(jnp.maximum, lses)
        scales = [jnp.exp2(line - peak) for line in lses]
        inverse = 1.0 / functools.reduce(jnp.add, scales)
        result = functools.reduce(
            jnp.add, [o * (scale * inverse) for o, scale in zip(outs, scales)]
        )
        result = jnp.transpose(result).astype(BF)
        for p in range(PER):
            out_ref[:, (g * PER + p) * HD:(g * PER + p + 1) * HD] = result[p * rows:(p + 1) * rows]

    previous = None
    done, finished = set(), set()
    for t, task in enumerate(tasks + [None]):
        if task is None and previous[2] > 0:
            src, g, k = previous
            pl.semaphore_signal(fence, inc=1)
            pl.semaphore_wait(fence, 1)
            finished.add((g, k))
            last_stage(g, k, 1 - t % 2)
        else:
            stage(task, previous, t % 2)
        if previous is not None:
            done.add(previous)
            for g in range(groups):
                for k in reversed(range(chunks)):
                    if k > 0 and (1, g, 0) in done and (0, g, k) in done and (g, k) not in finished:
                        finished.add((g, k))
                        finish(g, k)
        previous = task
    for g in range(groups):
        finish(g, 0)
    for g in range(groups):
        collect(g)
    for copy in q_copies.values():
        copy.wait_send()
    for _, _, copy in sent:
        copy.wait_send()


def on_device(
    queries, root_keys, root_values, branch_keys, branch_values, branch_lengths, row_branch
):
    rows = queries.shape[0]
    all_rows = row_branch.shape[0]
    n = all_rows // rows
    tokens, width = root_keys.shape
    groups = width // HD
    chunks = n // 2
    slots = 2 * rows
    cols = slots * PER
    part = rows * PER
    tb = min(TB, tokens)
    vmem = pl.BlockSpec(memory_space=pltpu.VMEM)
    hbm = pl.BlockSpec(memory_space=pl.ANY)
    dma = pltpu.SemaphoreType.DMA
    return pl.pallas_call(
        functools.partial(kernel, n, rows, tokens, groups, tb),
        out_shape=pltpu.VMEM(queries.shape, BF),
        in_specs=[hbm] * 7,
        out_specs=vmem,
        scratch_shapes=[
            pltpu.VMEM((n, rows, groups * PER * HD), BF),
            pltpu.VMEM((2, tokens, width), BF),
            pltpu.VMEM((2, tokens, width), BF),
            pltpu.VMEM((groups, HD, tokens), BF),
            pltpu.VMEM((tokens, cols), F32),
            pltpu.VMEM((tokens, cols), F32),
            pltpu.VMEM((CHAIN, cols), F32),
            pltpu.VMEM((CHAIN, cols), F32),
            pltpu.VMEM((groups, chunks, HD + STAT, cols), F32),
            pltpu.VMEM((groups, chunks, 8, cols), F32),
            pltpu.VMEM((groups, 2 * HD + STAT, cols), BF),
            pltpu.VMEM((n, cols, part), BF),
            pltpu.VMEM((1, all_rows), jnp.int32),
            pltpu.SMEM((1,), jnp.int32),
            pltpu.VMEM((groups, n, HD + STAT, part), BF),
            pltpu.VMEM((groups, n, HD + STAT, part), BF),
            dma((4,)), dma((3,)), pltpu.SemaphoreType.REGULAR, dma((groups, n)), dma((groups, n)),
            dma((groups, n)), dma((groups, n)),
        ],
        compiler_params=pltpu.CompilerParams(
            collective_id=0, has_side_effects=True, vmem_limit_bytes=60 * 1024 * 1024
        ),
        name="cascade",
    )(
        queries, row_branch.reshape(1, all_rows), branch_lengths,
        root_keys, root_values, branch_keys, branch_values,
    )


TB = 256


def solution(mesh):
    placed = (
        P(("groups", "branch"), "head"),
        P(("groups", "branch"), "head"),
        P(("groups", "branch"), "head"),
        P(("groups", "branch"), None, "head"),
        P(("groups", "branch"), None, "head"),
        P(("groups", "branch")),
        P("groups"),
    )
    return jax.shard_map(
        on_device,
        mesh=mesh,
        in_specs=placed,
        out_specs=P(("groups", "branch"), "head"),
        check_vma=False,
    )
```

```python
import functools
import math

import jax
import jax.numpy as jnp
from jax import lax
from jax.experimental import pallas as pl
from jax.experimental.pallas import tpu as pltpu
from jax.sharding import PartitionSpec as P

HD = 128
PER = 8
NEG = -1e30
STAT = 16
CHAIN = 32
MESH = pl.DeviceIdType.MESH
BF = jnp.bfloat16
F32 = jnp.float32
SPLIT_DIMS = (((1,), (1,)), ((), ()))


def split(value, parts):
    pieces = []
    for _ in range(parts):
        piece = value.astype(BF)
        pieces.append(piece)
        value = value - piece.astype(F32)
    return pieces


def kernel(
    n, rows, tokens, groups, tb,
    q_ref, rb_ref, len_ref, rk_ref, rv_ref, bk_ref, bv_ref, out_ref,
    qall, kbuf, vbuf, vt, bias, sbuf0, sbuf1, mbuf0, mbuf1, rnum, rm, right, place_e, rbuf, lbuf,
    send, recv,
    kv_sem, small_sem, fence, q_send, q_recv, o_send, o_recv,
):
    me = lax.axis_index("branch")
    slots = 2 * rows
    cols = slots * PER
    part = rows * PER
    chunks = n // 2
    span = min(512, tokens)
    all_rows = n * rows
    sbufs, mbufs = (sbuf0, sbuf1), (mbuf0, mbuf1)
    factor = math.log2(math.e) / math.sqrt(HD)

    copies = [
        pltpu.make_async_copy(src, dst, kv_sem.at[i])
        for i, (src, dst) in enumerate((
            (rk_ref, kbuf.at[0]), (rv_ref, vbuf.at[0]),
            (bk_ref.at[0], kbuf.at[1]), (bv_ref.at[0], vbuf.at[1]),
        ))
    ]
    own = pltpu.make_async_copy(q_ref, qall.at[me], small_sem.at[0])
    rb_copy = pltpu.make_async_copy(rb_ref, rbuf, small_sem.at[1])
    len_copy = pltpu.make_async_copy(len_ref, lbuf, small_sem.at[2])
    own.start()
    rb_copy.start()
    len_copy.start()
    copies[0].start()

    barrier = pltpu.get_barrier_semaphore()
    for off in range(1, n):
        peer = me ^ off
        pl.semaphore_signal(barrier, inc=1, device_id={"branch": peer}, device_id_type=MESH)
    copies[1].start()
    rb_copy.wait()
    len_copy.wait()
    rb = rbuf[...]
    mem_row = jnp.where(rb == me, 1.0, 0.0).astype(F32)
    r_sub = lax.broadcasted_iota(jnp.int32, (all_rows, all_rows), 0)
    r_lane = lax.broadcasted_iota(jnp.int32, (all_rows, all_rows), 1)
    mem_b = jnp.broadcast_to(mem_row, (all_rows, all_rows))
    mem_col = jnp.sum(jnp.where(r_sub == r_lane, mem_b, 0.0), axis=1, keepdims=True)
    mem_cb = jnp.broadcast_to(mem_col, (all_rows, all_rows))
    rank_row = jnp.sum(jnp.where(r_sub < r_lane, mem_cb, 0.0), axis=0, keepdims=True)
    slot_sub = lax.broadcasted_iota(jnp.int32, (slots, all_rows), 0).astype(F32)
    picker = jnp.where(
        (jnp.broadcast_to(rank_row, (slots, all_rows)) == slot_sub)
        & (jnp.broadcast_to(mem_row, (slots, all_rows)) > 0.5), 1.0, 0.0,
    ).astype(BF)
    sub = lax.broadcasted_iota(jnp.int32, (cols, part), 0)
    lane = lax.broadcasted_iota(jnp.int32, (cols, part), 1)
    same = (sub // slots) == (lane // rows)
    t_sub = lax.broadcasted_iota(jnp.int32, (all_rows, part), 0)
    t_lane = lax.broadcasted_iota(jnp.int32, (all_rows, part), 1)
    for d in range(n):
        spread = jnp.where(t_sub == d * rows + lax.rem(t_lane, rows), 1.0, 0.0).astype(BF)
        wide = jnp.dot(picker, spread, preferred_element_type=F32)
        wide = jnp.concatenate([wide] * PER, axis=0)
        place_e[d] = jnp.where(same, wide, 0.0).astype(BF)
    length = jnp.full((tb, HD), lbuf[0], jnp.int32)

    own.wait()
    pl.semaphore_wait(barrier, n - 1)

    q_copies = {}
    for g in range(groups):
        for off in reversed(range(1, n)):
            peer = me ^ off
            lanes = pl.ds(g * PER * HD, PER * HD)
            copy = pltpu.make_async_remote_copy(
                src_ref=qall.at[me, :, lanes], dst_ref=qall.at[me, :, lanes],
                send_sem=q_send.at[g, off], recv_sem=q_recv.at[g, off],
                device_id={"branch": peer}, device_id_type=MESH,
            )
            copy.start()
            q_copies[g, off] = copy
    copies[2].start()
    copies[3].start()

    for start in range(0, tokens, tb):
        place = start + lax.broadcasted_iota(jnp.int32, (tb, HD), 0)
        bias[start:start + tb] = jnp.where(place < length, 0.0, NEG)

    def stack(q):
        return jnp.concatenate([q[:, p * HD:(p + 1) * HD] for p in range(PER)], axis=0)

    tasks = [(0, g, 0) for g in range(groups)]
    for g in range(groups):
        tasks += [(1, g, 0)] + [(0, g, k) for k in range(1, chunks)]

    waited = set()

    def once(key, fn):
        if key not in waited:
            waited.add(key)
            fn()

    def need_q(g, off):
        if off > 0:
            once(("q", g, off), q_copies[g, off].wait_recv)

    def stage(first, second, slot):
        other = 1 - slot
        pl.semaphore_signal(fence, inc=1)
        pl.semaphore_wait(fence, 1)
        if first is not None:
            src, g, k = first
            lanes = slice(g * PER * HD, (g + 1) * PER * HD)
            once(2 * src, copies[2 * src].wait)
            if src == 0:
                need_q(g, 2 * k)
                need_q(g, 2 * k + 1)
                base = (me // 2) ^ k
                query = jnp.concatenate(
                    [stack(qall[base * 2 + i, :, lanes]) for i in range(2)], axis=0
                )
            else:
                for off in range(n):
                    need_q(g, off)
                whole = qall[:, :, lanes].reshape(all_rows, PER * HD)
                query = stack(jnp.dot(picker, whole, preferred_element_type=F32).astype(BF))
        run = jnp.full((CHAIN, cols), NEG, F32)
        total = jnp.zeros((HD + STAT, cols), F32)
        if second is not None:
            src2, g2, k2 = second
            once(2 * src2 + 1, copies[2 * src2 + 1].wait)
            peak = jnp.max(mbufs[other][...], axis=0, keepdims=True) * factor
            top = jnp.broadcast_to(peak, (8, cols))
            fresh = ("vt", src2, g2) not in waited

        for start in range(0, tokens, tb):
            tile = slice(start, start + tb)
            if first is not None:
                keys = kbuf[src, tile, g * HD:(g + 1) * HD]
                score = lax.dot_general(keys, query, SPLIT_DIMS, preferred_element_type=F32)
                score = score.reshape(tb // 8, 8, cols)
                if src == 1:
                    hide = bias[tile]
                    hide = jnp.concatenate([hide] * (cols // HD), axis=1)
                    score = score + hide.reshape(tb // 8, 8, cols)
                run = jnp.maximum(run, jnp.max(score.reshape(tb // CHAIN, CHAIN, cols), axis=0))
                sbufs[slot][tile] = score.reshape(tb, cols)
            if second is not None:
                s2 = sbufs[other][tile].reshape(tb // 8, 8, cols)
                weights = jnp.exp2(s2 * factor - top[None]).reshape(tb, cols).astype(BF)
                if fresh:
                    v = jnp.transpose(vbuf[src2, tile, g2 * HD:(g2 + 1) * HD])
                    if src2 == 0 and chunks > 1:
                        vt[g2, :, tile] = v
                else:
                    v = vt[g2, :, tile]
                left = jnp.concatenate([v, jnp.ones((STAT, tb), BF)], axis=0)
                total = total + jnp.dot(left, weights, preferred_element_type=F32)

        if first is not None:
            mbufs[slot][...] = run
        if second is not None:
            waited.add(("vt", src2, g2))
            if src2 == 0:
                rnum[g2, k2] = total
                rm[g2, k2] = top
            else:
                hi, lo = split(total[:HD], 2)
                stats = split(total[HD:HD + 1], 2) + split(peak, 3)
                stats += [jnp.zeros((1, cols), BF)] * (STAT - 5)
                right[g2] = jnp.concatenate([hi, lo] + stats, axis=0)

    sent = []

    def finish(g, k):
        base = (me // 2) ^ k
        e = jnp.concatenate([place_e[base * 2], place_e[base * 2 + 1]], axis=1)
        has = jnp.sum(e.astype(F32), axis=0, keepdims=True) > 0.5
        back = jnp.dot(right[g], e, preferred_element_type=F32)
        b_num = back[:HD] + back[HD:2 * HD]
        b_tot = back[2 * HD:2 * HD + 1] + back[2 * HD + 1:2 * HD + 2]
        b_top = back[2 * HD + 2:2 * HD + 3] + back[2 * HD + 3:2 * HD + 4] + back[2 * HD + 4:2 * HD + 5]
        b_top = jnp.where(has, b_top, NEG)
        r_num = rnum[g, k, :HD]
        r_tot = rnum[g, k, HD:HD + 1]
        r_top = rm[g, k, :1]
        peak = jnp.maximum(r_top, b_top)
        x = jnp.exp2(r_top - peak)
        y = jnp.exp2(b_top - peak)
        tot = r_tot * x + b_tot * y
        inverse = 1.0 / tot
        out = (r_num * (x * inverse) + b_num * (y * inverse)).astype(BF)
        lse = split(peak + jnp.log2(tot), 3)
        lse = jnp.concatenate(lse + [jnp.zeros((1, cols), BF)] * (STAT - 3), axis=0)
        for half in range(2):
            lo, hi = half * part, (half + 1) * part
            send[g, 2 * k + half, :HD] = out[:, lo:hi]
            send[g, 2 * k + half, HD:] = lse[:, lo:hi]
        for off in range(max(1, 2 * k), 2 * k + 2):
            peer = me ^ off
            index = 2 * k + lax.rem(peer, 2)
            copy = pltpu.make_async_remote_copy(
                src_ref=send.at[g, index], dst_ref=recv.at[g, off],
                send_sem=o_send.at[g, off], recv_sem=o_recv.at[g, off],
                device_id={"branch": peer}, device_id_type=MESH,
            )
            copy.start()
            sent.append((g, off, copy))

    def last_stage(g, k, other):
        for off in (2 * k, 2 * k + 1):
            peer = me ^ off
            lanes = pl.ds(pl.multiple_of(lax.rem(peer, 2) * part, part), part)
            r_top = jnp.max(mbufs[other][:, lanes], axis=0, keepdims=True) * factor
            top = jnp.broadcast_to(r_top, (8, part))
            total = jnp.zeros((HD + STAT, part), F32)
            for start in range(0, tokens, span):
                tile = slice(start, start + span)
                s2 = sbufs[other][tile, lanes].reshape(span // 8, 8, part)
                weights = jnp.exp2(s2 * factor - top[None]).reshape(span, part).astype(BF)
                left = jnp.concatenate([vt[g, :, tile], jnp.ones((STAT, span), BF)], axis=0)
                total = total + jnp.dot(left, weights, preferred_element_type=F32)
            e = place_e[peer]
            has = jnp.sum(e.astype(F32), axis=0, keepdims=True) > 0.5
            back = jnp.dot(right[g], e, preferred_element_type=F32)
            b_num = back[:HD] + back[HD:2 * HD]
            b_tot = back[2 * HD:2 * HD + 1] + back[2 * HD + 1:2 * HD + 2]
            b_top = back[2 * HD + 2:2 * HD + 3] + back[2 * HD + 3:2 * HD + 4] + back[2 * HD + 4:2 * HD + 5]
            b_top = jnp.where(has, b_top, NEG)
            peak = jnp.maximum(r_top, b_top)
            x = jnp.exp2(r_top - peak)
            y = jnp.exp2(b_top - peak)
            tot = total[HD:HD + 1] * x + b_tot * y
            inverse = 1.0 / tot
            out = (total[:HD] * (x * inverse) + b_num * (y * inverse)).astype(BF)
            lse = split(peak + jnp.log2(tot), 3)
            lse = jnp.concatenate(lse + [jnp.zeros((1, part), BF)] * (STAT - 3), axis=0)
            send[g, off, :HD] = out
            send[g, off, HD:] = lse
            copy = pltpu.make_async_remote_copy(
                src_ref=send.at[g, off], dst_ref=recv.at[g, off],
                send_sem=o_send.at[g, off], recv_sem=o_recv.at[g, off],
                device_id={"branch": peer}, device_id_type=MESH,
            )
            copy.start()
            sent.append((g, off, copy))
            pl.semaphore_signal(fence, inc=1)
            pl.semaphore_wait(fence, 1)

    def collect(g):
        blocks_in = [send[g, lax.rem(me, 2)]]
        for gg, off, copy in sent:
            if gg == g:
                copy.wait_recv()
                blocks_in.append(recv[g, off])
        lses, outs = [], []
        for block in blocks_in:
            stat = block[HD:].astype(F32)
            lses.append(stat[0:1] + stat[1:2] + stat[2:3])
            outs.append(block[:HD].astype(F32))
        peak = functools.reduce(jnp.maximum, lses)
        scales = [jnp.exp2(line - peak) for line in lses]
        inverse = 1.0 / functools.reduce(jnp.add, scales)
        result = functools.reduce(
            jnp.add, [o * (scale * inverse) for o, scale in zip(outs, scales)]
        )
        result = jnp.transpose(result).astype(BF)
        for p in range(PER):
            out_ref[:, (g * PER + p) * HD:(g * PER + p + 1) * HD] = result[p * rows:(p + 1) * rows]

    previous = None
    done, finished = set(), set()
    for t, task in enumerate(tasks + [None]):
        if task is None and previous[2] > 0:
            src, g, k = previous
            pl.semaphore_signal(fence, inc=1)
            pl.semaphore_wait(fence, 1)
            finished.add((g, k))
            last_stage(g, k, 1 - t % 2)
        else:
            stage(task, previous, t % 2)
        if previous is not None:
            done.add(previous)
            for g in range(groups):
                for k in reversed(range(chunks)):
                    if k > 0 and (1, g, 0) in done and (0, g, k) in done and (g, k) not in finished:
                        finished.add((g, k))
                        finish(g, k)
        previous = task
    for g in range(groups):
        finish(g, 0)
    for g in range(groups):
        collect(g)
    for copy in q_copies.values():
        copy.wait_send()
    for _, _, copy in sent:
        copy.wait_send()


def on_device(
    queries, root_keys, root_values, branch_keys, branch_values, branch_lengths, row_branch
):
    rows = queries.shape[0]
    all_rows = row_branch.shape[0]
    n = all_rows // rows
    tokens, width = root_keys.shape
    groups = width // HD
    chunks = n // 2
    slots = 2 * rows
    cols = slots * PER
    part = rows * PER
    tb = min(TB, tokens)
    vmem = pl.BlockSpec(memory_space=pltpu.VMEM)
    hbm = pl.BlockSpec(memory_space=pl.ANY)
    dma = pltpu.SemaphoreType.DMA
    return pl.pallas_call(
        functools.partial(kernel, n, rows, tokens, groups, tb),
        out_shape=pltpu.VMEM(queries.shape, BF),
        in_specs=[hbm] * 7,
        out_specs=vmem,
        scratch_shapes=[
            pltpu.VMEM((n, rows, groups * PER * HD), BF),
            pltpu.VMEM((2, tokens, width), BF),
            pltpu.VMEM((2, tokens, width), BF),
            pltpu.VMEM((groups, HD, tokens), BF),
            pltpu.VMEM((tokens, HD), F32),
            pltpu.VMEM((tokens, cols), F32),
            pltpu.VMEM((tokens, cols), F32),
            pltpu.VMEM((CHAIN, cols), F32),
            pltpu.VMEM((CHAIN, cols), F32),
            pltpu.VMEM((groups, chunks, HD + STAT, cols), F32),
            pltpu.VMEM((groups, chunks, 8, cols), F32),
            pltpu.VMEM((groups, 2 * HD + STAT, cols), BF),
            pltpu.VMEM((n, cols, part), BF),
            pltpu.VMEM((1, all_rows), jnp.int32),
            pltpu.SMEM((1,), jnp.int32),
            pltpu.VMEM((groups, n, HD + STAT, part), BF),
            pltpu.VMEM((groups, n, HD + STAT, part), BF),
            dma((4,)), dma((3,)), pltpu.SemaphoreType.REGULAR, dma((groups, n)), dma((groups, n)),
            dma((groups, n)), dma((groups, n)),
        ],
        compiler_params=pltpu.CompilerParams(
            collective_id=0, has_side_effects=True, vmem_limit_bytes=60 * 1024 * 1024
        ),
        name="cascade",
    )(
        queries, row_branch.reshape(1, all_rows), branch_lengths,
        root_keys, root_values, branch_keys, branch_values,
    )


TB = 256


def solution(mesh):
    placed = (
        P(("groups", "branch"), "head"),
        P(("groups", "branch"), "head"),
        P(("groups", "branch"), "head"),
        P(("groups", "branch"), None, "head"),
        P(("groups", "branch"), None, "head"),
        P(("groups", "branch")),
        P("groups"),
    )
    return jax.shard_map(
        on_device,
        mesh=mesh,
        in_specs=placed,
        out_specs=P(("groups", "branch"), "head"),
        check_vma=False,
    )
```

```python
import functools
import math

import jax
import jax.numpy as jnp
from jax import lax
from jax.experimental import pallas as pl
from jax.experimental.pallas import tpu as pltpu
from jax.sharding import PartitionSpec as P

HD = 128
PER = 8
NEG = -1e30
STAT = 16
CHAIN = 32
MESH = pl.DeviceIdType.MESH
BF = jnp.bfloat16
F32 = jnp.float32
SPLIT_DIMS = (((1,), (1,)), ((), ()))


def split(value, parts):
    pieces = []
    for _ in range(parts):
        piece = value.astype(BF)
        pieces.append(piece)
        value = value - piece.astype(F32)
    return pieces


def kernel(
    n, rows, tokens, groups, tb,
    q_ref, rb_ref, len_ref, rk_ref, rv_ref, bk_ref, bv_ref, out_ref,
    qall, kbuf, vbuf, vt, bias, sbuf0, sbuf1, mbuf0, mbuf1, rnum, rm, right, place_e, rbuf, lbuf,
    send, recv,
    kv_sem, small_sem, fence, q_send, q_recv, o_send, o_recv,
):
    me = lax.axis_index("branch")
    slots = 2 * rows
    cols = slots * PER
    part = rows * PER
    chunks = n // 2
    span = min(512, tokens)
    all_rows = n * rows
    sbufs, mbufs = (sbuf0, sbuf1), (mbuf0, mbuf1)
    factor = math.log2(math.e) / math.sqrt(HD)

    barrier = pltpu.get_barrier_semaphore()
    for off in reversed(range(1, n)):
        peer = me ^ off
        pl.semaphore_signal(barrier, inc=1, device_id={"branch": peer}, device_id_type=MESH)

    copies = [
        pltpu.make_async_copy(src, dst, kv_sem.at[i])
        for i, (src, dst) in enumerate((
            (rk_ref, kbuf.at[0]), (rv_ref, vbuf.at[0]),
            (bk_ref.at[0], kbuf.at[1]), (bv_ref.at[0], vbuf.at[1]),
        ))
    ]
    own = pltpu.make_async_copy(q_ref, qall.at[me], small_sem.at[0])
    rb_copy = pltpu.make_async_copy(rb_ref, rbuf, small_sem.at[1])
    len_copy = pltpu.make_async_copy(len_ref, lbuf, small_sem.at[2])
    own.start()
    rb_copy.start()
    len_copy.start()
    copies[0].start()

    copies[1].start()
    rb_copy.wait()
    len_copy.wait()
    rb = rbuf[...]
    mem_row = jnp.where(rb == me, 1.0, 0.0).astype(F32)
    r_sub = lax.broadcasted_iota(jnp.int32, (all_rows, all_rows), 0)
    r_lane = lax.broadcasted_iota(jnp.int32, (all_rows, all_rows), 1)
    mem_b = jnp.broadcast_to(mem_row, (all_rows, all_rows))
    mem_col = jnp.sum(jnp.where(r_sub == r_lane, mem_b, 0.0), axis=1, keepdims=True)
    mem_cb = jnp.broadcast_to(mem_col, (all_rows, all_rows))
    rank_row = jnp.sum(jnp.where(r_sub < r_lane, mem_cb, 0.0), axis=0, keepdims=True)
    slot_sub = lax.broadcasted_iota(jnp.int32, (slots, all_rows), 0).astype(F32)
    picker = jnp.where(
        (jnp.broadcast_to(rank_row, (slots, all_rows)) == slot_sub)
        & (jnp.broadcast_to(mem_row, (slots, all_rows)) > 0.5), 1.0, 0.0,
    ).astype(BF)
    sub = lax.broadcasted_iota(jnp.int32, (cols, part), 0)
    lane = lax.broadcasted_iota(jnp.int32, (cols, part), 1)
    same = (sub // slots) == (lane // rows)
    t_sub = lax.broadcasted_iota(jnp.int32, (all_rows, part), 0)
    t_lane = lax.broadcasted_iota(jnp.int32, (all_rows, part), 1)
    for d in range(n):
        spread = jnp.where(t_sub == d * rows + lax.rem(t_lane, rows), 1.0, 0.0).astype(BF)
        wide = jnp.dot(picker, spread, preferred_element_type=F32)
        wide = jnp.concatenate([wide] * PER, axis=0)
        place_e[d] = jnp.where(same, wide, 0.0).astype(BF)
    length = jnp.full((tb, HD), lbuf[0], jnp.int32)

    own.wait()
    pl.semaphore_wait(barrier, n - 1)

    q_copies = {}
    for g in range(groups):
        for off in reversed(range(1, n)):
            peer = me ^ off
            lanes = pl.ds(g * PER * HD, PER * HD)
            copy = pltpu.make_async_remote_copy(
                src_ref=qall.at[me, :, lanes], dst_ref=qall.at[me, :, lanes],
                send_sem=q_send.at[g, off], recv_sem=q_recv.at[g, off],
                device_id={"branch": peer}, device_id_type=MESH,
            )
            copy.start()
            q_copies[g, off] = copy
    copies[2].start()
    copies[3].start()

    for start in range(0, tokens, tb):
        place = start + lax.broadcasted_iota(jnp.int32, (tb, HD), 0)
        bias[start:start + tb] = jnp.where(place < length, 0.0, NEG)

    def stack(q):
        return jnp.concatenate([q[:, p * HD:(p + 1) * HD] for p in range(PER)], axis=0)

    tasks = [(0, g, 0) for g in range(groups)]
    for g in range(groups):
        tasks += [(1, g, 0)] + [(0, g, k) for k in range(1, chunks)]

    waited = set()

    def once(key, fn):
        if key not in waited:
            waited.add(key)
            fn()

    def need_q(g, off):
        if off > 0:
            once(("q", g, off), q_copies[g, off].wait_recv)

    def stage(first, second, slot):
        other = 1 - slot
        pl.semaphore_signal(fence, inc=1)
        pl.semaphore_wait(fence, 1)
        if first is not None:
            src, g, k = first
            lanes = slice(g * PER * HD, (g + 1) * PER * HD)
            once(2 * src, copies[2 * src].wait)
            if src == 0:
                need_q(g, 2 * k)
                need_q(g, 2 * k + 1)
                base = (me // 2) ^ k
                query = jnp.concatenate(
                    [stack(qall[base * 2 + i, :, lanes]) for i in range(2)], axis=0
                )
            else:
                for off in range(n):
                    need_q(g, off)
                whole = qall[:, :, lanes].reshape(all_rows, PER * HD)
                query = stack(jnp.dot(picker, whole, preferred_element_type=F32).astype(BF))
        run = jnp.full((CHAIN, cols), NEG, F32)
        total = jnp.zeros((HD + STAT, cols), F32)
        if second is not None:
            src2, g2, k2 = second
            once(2 * src2 + 1, copies[2 * src2 + 1].wait)
            peak = jnp.max(mbufs[other][...], axis=0, keepdims=True) * factor
            top = jnp.broadcast_to(peak, (8, cols))
            fresh = ("vt", src2, g2) not in waited

        for start in range(0, tokens, tb):
            tile = slice(start, start + tb)
            if first is not None:
                keys = kbuf[src, tile, g * HD:(g + 1) * HD]
                score = lax.dot_general(keys, query, SPLIT_DIMS, preferred_element_type=F32)
                score = score.reshape(tb // 8, 8, cols)
                if src == 1:
                    hide = bias[tile]
                    hide = jnp.concatenate([hide] * (cols // HD), axis=1)
                    score = score + hide.reshape(tb // 8, 8, cols)
                run = jnp.maximum(run, jnp.max(score.reshape(tb // CHAIN, CHAIN, cols), axis=0))
                sbufs[slot][tile] = score.reshape(tb, cols)
            if second is not None:
                s2 = sbufs[other][tile].reshape(tb // 8, 8, cols)
                weights = jnp.exp2(s2 * factor - top[None]).reshape(tb, cols).astype(BF)
                if fresh:
                    v = jnp.transpose(vbuf[src2, tile, g2 * HD:(g2 + 1) * HD])
                    if src2 == 0 and chunks > 1:
                        vt[g2, :, tile] = v
                else:
                    v = vt[g2, :, tile]
                left = jnp.concatenate([v, jnp.ones((STAT, tb), BF)], axis=0)
                total = total + jnp.dot(left, weights, preferred_element_type=F32)

        if first is not None:
            mbufs[slot][...] = run
        if second is not None:
            waited.add(("vt", src2, g2))
            if src2 == 0:
                rnum[g2, k2] = total
                rm[g2, k2] = top
            else:
                hi, lo = split(total[:HD], 2)
                stats = split(total[HD:HD + 1], 2) + split(peak, 3)
                stats += [jnp.zeros((1, cols), BF)] * (STAT - 5)
                right[g2] = jnp.concatenate([hi, lo] + stats, axis=0)

    sent = []

    def finish(g, k):
        base = (me // 2) ^ k
        e = jnp.concatenate([place_e[base * 2], place_e[base * 2 + 1]], axis=1)
        has = jnp.sum(e.astype(F32), axis=0, keepdims=True) > 0.5
        back = jnp.dot(right[g], e, preferred_element_type=F32)
        b_num = back[:HD] + back[HD:2 * HD]
        b_tot = back[2 * HD:2 * HD + 1] + back[2 * HD + 1:2 * HD + 2]
        b_top = back[2 * HD + 2:2 * HD + 3] + back[2 * HD + 3:2 * HD + 4] + back[2 * HD + 4:2 * HD + 5]
        b_top = jnp.where(has, b_top, NEG)
        r_num = rnum[g, k, :HD]
        r_tot = rnum[g, k, HD:HD + 1]
        r_top = rm[g, k, :1]
        peak = jnp.maximum(r_top, b_top)
        x = jnp.exp2(r_top - peak)
        y = jnp.exp2(b_top - peak)
        tot = r_tot * x + b_tot * y
        inverse = 1.0 / tot
        out = (r_num * (x * inverse) + b_num * (y * inverse)).astype(BF)
        lse = split(peak + jnp.log2(tot), 3)
        lse = jnp.concatenate(lse + [jnp.zeros((1, cols), BF)] * (STAT - 3), axis=0)
        for half in range(2):
            lo, hi = half * part, (half + 1) * part
            send[g, 2 * k + half, :HD] = out[:, lo:hi]
            send[g, 2 * k + half, HD:] = lse[:, lo:hi]
        for off in range(max(1, 2 * k), 2 * k + 2):
            peer = me ^ off
            index = 2 * k + lax.rem(peer, 2)
            copy = pltpu.make_async_remote_copy(
                src_ref=send.at[g, index], dst_ref=recv.at[g, off],
                send_sem=o_send.at[g, off], recv_sem=o_recv.at[g, off],
                device_id={"branch": peer}, device_id_type=MESH,
            )
            copy.start()
            sent.append((g, off, copy))

    def last_stage(g, k, other):
        for off in (2 * k, 2 * k + 1):
            peer = me ^ off
            lanes = pl.ds(pl.multiple_of(lax.rem(peer, 2) * part, part), part)
            r_top = jnp.max(mbufs[other][:, lanes], axis=0, keepdims=True) * factor
            top = jnp.broadcast_to(r_top, (8, part))
            total = jnp.zeros((HD + STAT, part), F32)
            for start in range(0, tokens, span):
                tile = slice(start, start + span)
                s2 = sbufs[other][tile, lanes].reshape(span // 8, 8, part)
                weights = jnp.exp2(s2 * factor - top[None]).reshape(span, part).astype(BF)
                left = jnp.concatenate([vt[g, :, tile], jnp.ones((STAT, span), BF)], axis=0)
                total = total + jnp.dot(left, weights, preferred_element_type=F32)
            e = place_e[peer]
            has = jnp.sum(e.astype(F32), axis=0, keepdims=True) > 0.5
            back = jnp.dot(right[g], e, preferred_element_type=F32)
            b_num = back[:HD] + back[HD:2 * HD]
            b_tot = back[2 * HD:2 * HD + 1] + back[2 * HD + 1:2 * HD + 2]
            b_top = back[2 * HD + 2:2 * HD + 3] + back[2 * HD + 3:2 * HD + 4] + back[2 * HD + 4:2 * HD + 5]
            b_top = jnp.where(has, b_top, NEG)
            peak = jnp.maximum(r_top, b_top)
            x = jnp.exp2(r_top - peak)
            y = jnp.exp2(b_top - peak)
            tot = total[HD:HD + 1] * x + b_tot * y
            inverse = 1.0 / tot
            out = (total[:HD] * (x * inverse) + b_num * (y * inverse)).astype(BF)
            lse = split(peak + jnp.log2(tot), 3)
            lse = jnp.concatenate(lse + [jnp.zeros((1, part), BF)] * (STAT - 3), axis=0)
            send[g, off, :HD] = out
            send[g, off, HD:] = lse
            copy = pltpu.make_async_remote_copy(
                src_ref=send.at[g, off], dst_ref=recv.at[g, off],
                send_sem=o_send.at[g, off], recv_sem=o_recv.at[g, off],
                device_id={"branch": peer}, device_id_type=MESH,
            )
            copy.start()
            sent.append((g, off, copy))
            pl.semaphore_signal(fence, inc=1)
            pl.semaphore_wait(fence, 1)

    def collect(g):
        blocks_in = [send[g, lax.rem(me, 2)]]
        for gg, off, copy in sent:
            if gg == g:
                copy.wait_recv()
                blocks_in.append(recv[g, off])
        lses, outs = [], []
        for block in blocks_in:
            stat = block[HD:].astype(F32)
            lses.append(stat[0:1] + stat[1:2] + stat[2:3])
            outs.append(block[:HD].astype(F32))
        peak = functools.reduce(jnp.maximum, lses)
        scales = [jnp.exp2(line - peak) for line in lses]
        inverse = 1.0 / functools.reduce(jnp.add, scales)
        result = functools.reduce(
            jnp.add, [o * (scale * inverse) for o, scale in zip(outs, scales)]
        )
        result = jnp.transpose(result).astype(BF)
        for p in range(PER):
            out_ref[:, (g * PER + p) * HD:(g * PER + p + 1) * HD] = result[p * rows:(p + 1) * rows]

    previous = None
    done, finished = set(), set()
    for t, task in enumerate(tasks + [None]):
        if task is None and previous[2] > 0:
            src, g, k = previous
            pl.semaphore_signal(fence, inc=1)
            pl.semaphore_wait(fence, 1)
            finished.add((g, k))
            last_stage(g, k, 1 - t % 2)
        else:
            stage(task, previous, t % 2)
        if previous is not None:
            done.add(previous)
            for g in range(groups):
                for k in reversed(range(chunks)):
                    if k > 0 and (1, g, 0) in done and (0, g, k) in done and (g, k) not in finished:
                        finished.add((g, k))
                        finish(g, k)
        previous = task
    for g in range(groups):
        finish(g, 0)
    for g in range(groups):
        collect(g)
    for copy in q_copies.values():
        copy.wait_send()
    for _, _, copy in sent:
        copy.wait_send()


def on_device(
    queries, root_keys, root_values, branch_keys, branch_values, branch_lengths, row_branch
):
    rows = queries.shape[0]
    all_rows = row_branch.shape[0]
    n = all_rows // rows
    tokens, width = root_keys.shape
    groups = width // HD
    chunks = n // 2
    slots = 2 * rows
    cols = slots * PER
    part = rows * PER
    tb = min(TB, tokens)
    vmem = pl.BlockSpec(memory_space=pltpu.VMEM)
    hbm = pl.BlockSpec(memory_space=pl.ANY)
    dma = pltpu.SemaphoreType.DMA
    return pl.pallas_call(
        functools.partial(kernel, n, rows, tokens, groups, tb),
        out_shape=pltpu.VMEM(queries.shape, BF),
        in_specs=[hbm] * 7,
        out_specs=vmem,
        scratch_shapes=[
            pltpu.VMEM((n, rows, groups * PER * HD), BF),
            pltpu.VMEM((2, tokens, width), BF),
            pltpu.VMEM((2, tokens, width), BF),
            pltpu.VMEM((groups, HD, tokens), BF),
            pltpu.VMEM((tokens, HD), F32),
            pltpu.VMEM((tokens, cols), F32),
            pltpu.VMEM((tokens, cols), F32),
            pltpu.VMEM((CHAIN, cols), F32),
            pltpu.VMEM((CHAIN, cols), F32),
            pltpu.VMEM((groups, chunks, HD + STAT, cols), F32),
            pltpu.VMEM((groups, chunks, 8, cols), F32),
            pltpu.VMEM((groups, 2 * HD + STAT, cols), BF),
            pltpu.VMEM((n, cols, part), BF),
            pltpu.VMEM((1, all_rows), jnp.int32),
            pltpu.SMEM((1,), jnp.int32),
            pltpu.VMEM((groups, n, HD + STAT, part), BF),
            pltpu.VMEM((groups, n, HD + STAT, part), BF),
            dma((4,)), dma((3,)), pltpu.SemaphoreType.REGULAR, dma((groups, n)), dma((groups, n)),
            dma((groups, n)), dma((groups, n)),
        ],
        compiler_params=pltpu.CompilerParams(
            collective_id=0, has_side_effects=True, vmem_limit_bytes=60 * 1024 * 1024
        ),
        name="cascade",
    )(
        queries, row_branch.reshape(1, all_rows), branch_lengths,
        root_keys, root_values, branch_keys, branch_values,
    )


TB = 256


def solution(mesh):
    placed = (
        P(("groups", "branch"), "head"),
        P(("groups", "branch"), "head"),
        P(("groups", "branch"), "head"),
        P(("groups", "branch"), None, "head"),
        P(("groups", "branch"), None, "head"),
        P(("groups", "branch")),
        P("groups"),
    )
    return jax.shard_map(
        on_device,
        mesh=mesh,
        in_specs=placed,
        out_specs=P(("groups", "branch"), "head"),
        check_vma=False,
    )
```
